256 devices in a mesh: dp: 64 (over z, x, core), tp: 4 (over y).
Axes of the slice: x: 4, y: 4, z: 8, core: 2. Of those that a mesh axis runs over, the one named last changes fastest.
Arguments:
- queries: bfloat16 [4096, 73728], P('dp', 'tp'), may hold values from -32 to 32
- prefix_cache: bfloat16 [64, 576, 1024], P('dp', None, 'tp'), may hold values from -12 to 12
- suffix_cache: bfloat16 [4096, 576, 128], P('dp'), may hold values from -48 to 48
- w_uv: bfloat16 [128, 512, 128], P('tp'), may hold values from -1 to 1
- fork_prompt: int32 [4096, 1], P('dp'), may hold values from 0 to 63; in each aligned block of 64 rows (0 to 63, 64 to 127, ...) at most 2 rows name the same one
- prompt_slot: int32 [64], replicated, may hold values from 0 to 63, each once
- suffix_len: int32 [4096], P('dp'), may hold values from 32 to 128
Outputs:
- attended: bfloat16 [4096, 16384], P('dp', 'tp')
The draws below stay inside these ranges and needn't reach their ends.
Inputs may be any that keep to these rules, and one draw needn't show every extreme that they name: `fork_prompt`: among the 64 forks of one index of dp no prompt is named more than 2 times. `prompt_slot`: each slot holds exactly one prompt.
All inputs are finite; a program needn't handle non-finite values.
Results may differ from the reference program's by a relative error of at most 0.033.
Values may be sent and summed in bfloat16 or wider, within the bound.
No kernel may reach another device: no remote copies, remote signals or barrier semaphores. Data moves between devices by JAX's collectives and lax.ppermute only.
A program may use at most 128 MiB of HBM per device.

```python
import math
import jax
import jax.numpy as jnp
import numpy as np
from jax import lax

H = 128
R = 512
P_SIZE = 64
V = 128
L = 1024
S = 128
FORK_DEV = 64
MOST = 2
PROMPTS = 64
FORKS = 4096


def fork_pair(key):
    base = jax.random.fold_in(key, 7001)
    streams = jax.random.split(base, 2)
    key_width = R + P_SIZE
    suffix = jnp.clip(jax.random.normal(streams[0], (FORKS, key_width, S), jnp.float32), -4.0, 4.0)
    query = jnp.clip(jax.random.normal(streams[1], (FORKS, H, key_width), jnp.float32), -4.0, 4.0)
    suffix = jnp.clip(suffix, -48.0, 48.0)
    query = jnp.clip(query, -32.0, 32.0)
    return (query, suffix)


def draw_queries(key, part):
    query, suffix = fork_pair(key)
    return query.reshape(FORKS, H * (R + P_SIZE)).astype(jnp.bfloat16)


def draw_suffix_cache(key, part):
    query, suffix = fork_pair(key)
    return suffix.astype(jnp.bfloat16)


def draw_prefix_cache(key, part):
    base = jax.random.fold_in(key, 7002)
    streams = jax.random.split(base, 1)
    cache = jnp.clip(jax.random.normal(streams[0], (PROMPTS, R + P_SIZE, L), jnp.float32), -4.0, 4.0)
    return cache.astype(jnp.bfloat16)


def set_ends(values, key, low, high):
    longest = values.shape.index(max(values.shape))
    spots = []
    for shift in (0, 1):
        where = [jax.random.randint(jax.random.fold_in(key, axis), (), 0, length) for axis, length in enumerate(values.shape)]
        where[longest] = (where[longest] + shift) % values.shape[longest]
        spots.append(tuple(where))
    return values.at[spots[0]].set(low).at[spots[1]].set(high)


def shard_levels(stream_key, shape, shards, low, high):
    def one(axis_at, parts):
        steps = jax.random.uniform(jax.random.fold_in(jax.random.fold_in(stream_key, 6), axis_at), (parts,), jnp.float32, low / len(shards), high / len(shards))
        return jnp.repeat(jnp.exp(steps), shape[axis_at] // parts).reshape((-1,) + (1,) * (len(shape) - axis_at - 1))

    level = one(*shards[0])
    for cut in shards[1:]:
        level = level * one(*cut)
    return level


def shared_out(rng, own, number, rows, number_of, top, bound, skew):
    sequence = jax.random.permutation(rng, number_of)
    packed, common = portions_of(number_of, rows * top, bound, skew, True), portions_of(number_of, rows * top, bound, skew, False)
    places = jnp.arange(number_of)

    def named(lengths, rotation):
        used = int((lengths > 0).sum())
        fixed = max(1, used // 4)
        moved = fixed + (places - fixed + rotation * (used - fixed)) % max(1, number_of - fixed)
        return jnp.zeros((number_of,), jnp.int32).at[sequence[jnp.where(places < fixed, places, moved)]].set(jnp.asarray(lengths, jnp.int32))

    lengths = jnp.where(number % 4 == 0, named(packed, number // 4), named(common, number - number // 4 - 1))
    mixed = jax.random.permutation(jax.random.fold_in(own, 3), number_of)
    source_of, sink = mixed[0:number_of // 2 * 2:2], mixed[1:number_of // 2 * 2:2]
    slack = jnp.minimum(lengths[source_of] - 1, bound - lengths[sink]) // 2
    slack = jnp.where((source_of == sequence[0]) | (sink == sequence[0]) | (lengths[sink] == 0), 0, jnp.maximum(slack, 0))
    moved = jax.random.randint(jax.random.fold_in(own, 4), (number_of // 2,), 0, 1 << 20) % (slack + 1)
    lengths = lengths.at[source_of].add(-moved).at[sink].add(moved)
    members = jnp.searchsorted(jnp.cumsum(lengths), jnp.arange(rows * top), side="right").astype(jnp.int32)
    table = members.reshape(top, rows).T
    table = table[jax.random.permutation(jax.random.fold_in(own, 1), rows)]
    rotation = jax.random.randint(jax.random.fold_in(own, 2), (rows, 1), 0, top)
    return jnp.take_along_axis(table, (jnp.arange(top)[None, :] + rotation) % top, axis=1)


def portions_of(amount, total, bound, slope, full):
    weights = [(1 << 20) // math.isqrt(standing ** slope) + 1 for standing in range(1, amount + 1)]
    largest = bound if full else min(bound, max(-(-total // amount), total * weights[0] // sum(weights)))
    least = 1 if total - largest >= amount - 1 else 0
    counts, rest = [largest] + [least] * (amount - 1), total - largest - least * (amount - 1)
    while rest > 0:
        movable = [i for i in range(1, amount) if counts[i] < largest] or [i for i in range(1, amount) if counts[i] < bound]
        pool, budget = sum([weights[i] for i in movable]), rest
        for i in movable:
            more = min(bound - counts[i], max(1, budget * weights[i] // pool), rest)
            counts[i] = counts[i] + more
            rest = rest - more
    return np.array(counts)


def normal_values(own_key, dims, scale, most, pieces=(), kind=jnp.bfloat16):
    values = scale * jax.random.normal(own_key, dims, jnp.float32)
    if pieces:
        values = values * shard_levels(own_key, dims, pieces, -0.22, 0.18)
    return jnp.clip(values, -most, most).astype(kind)


def setup_inputs(seed: int = 0) -> dict:
    arg_keys = jax.random.split(jax.random.key(seed), 8)
    queries = draw_queries(jax.random.fold_in(arg_keys[7], 71), 0)
    prefix_cache = draw_prefix_cache(jax.random.fold_in(arg_keys[7], 71), 0)
    suffix_cache = draw_suffix_cache(jax.random.fold_in(arg_keys[7], 71), 0)
    w_uv = normal_values(arg_keys[3], (H, R, V), (R // 16) ** -0.5, 1.0, ((0, 4),))
    fork_prompt_keys = jax.random.split(jax.random.fold_in(arg_keys[4], 1), FORKS // FORK_DEV)
    fork_prompt_turns = jax.random.permutation(jax.random.fold_in(arg_keys[4], 3), FORKS // FORK_DEV)
    fork_prompt = jax.vmap(lambda own, number: shared_out(jax.random.fold_in(arg_keys[4], 2), own, number, FORK_DEV, PROMPTS, 1, MOST, 2))(fork_prompt_keys, fork_prompt_turns).reshape((FORKS, 1))
    prompt_slot = jax.random.permutation(arg_keys[5], PROMPTS).astype(jnp.int32)
    suffix_len = set_ends(jax.random.randint(arg_keys[6], (FORKS,), S // 4, S + 1), jax.random.fold_in(arg_keys[6], 1), S // 4, S).astype(jnp.int32)
    return {"queries": queries, "prefix_cache": prefix_cache, "suffix_cache": suffix_cache, "w_uv": w_uv, "fork_prompt": fork_prompt, "prompt_slot": prompt_slot, "suffix_len": suffix_len}


score_scale = 192.0 ** -0.5


def attend(query_heads, keys, live_mask):
    scores = jnp.einsum('bhe,bek->bhk', query_heads, keys) * score_scale
    scores = jnp.where(live_mask, scores, -jnp.inf)
    peak = jnp.max(scores, axis=2, keepdims=True)
    weights = jnp.where(live_mask, jnp.exp(scores - peak), 0.0)
    mass_sum = jnp.sum(weights, axis=2)
    rounded = lax.optimization_barrier(weights.astype(jnp.bfloat16)).astype(jnp.float32)
    summed = jnp.einsum('bhk,brk->bhr', rounded, keys[:, :R, :])
    latent = (summed / mass_sum[..., None]).astype(jnp.bfloat16)
    return latent, peak[..., 0] + jnp.log(mass_sum)


def project(latent, w_full):
    return jnp.einsum('bhr,hrv->bhv', latent.astype(jnp.float32), w_full).astype(jnp.bfloat16)


def reference(queries, prefix_cache, suffix_cache, w_uv, fork_prompt, prompt_slot, suffix_len):
    owner_slot = jnp.take(prompt_slot, fork_prompt[:, 0]).astype(jnp.int32)
    blocks = FORKS // FORK_DEV
    w_full = w_uv.astype(jnp.float32)

    def one_block(items):
        block_queries, block_suffix, block_owner, block_lengths = items
        query_heads = block_queries.astype(jnp.float32).reshape(FORK_DEV, H, R + P_SIZE)
        prefix_keys = jnp.take(prefix_cache, block_owner, axis=0).astype(jnp.float32)
        all_live = jnp.ones((FORK_DEV, 1, L), dtype=bool)
        latent_prefix, mass_prefix = attend(query_heads, prefix_keys, all_live)
        positions = jnp.arange(S).astype(jnp.int32)
        suffix_live = (positions[None, :] < block_lengths[:, None])[:, None, :]
        latent_suffix, mass_suffix = attend(query_heads, block_suffix.astype(jnp.float32), suffix_live)
        value_prefix = project(latent_prefix, w_full).astype(jnp.float32)
        value_suffix = project(latent_suffix, w_full).astype(jnp.float32)
        top_mass = jnp.maximum(mass_prefix, mass_suffix)
        share_prefix = jnp.exp(mass_prefix - top_mass)[..., None]
        share_suffix = jnp.exp(mass_suffix - top_mass)[..., None]
        combined = (share_prefix * value_prefix + share_suffix * value_suffix) / (share_prefix + share_suffix)
        return combined.astype(jnp.bfloat16).reshape(FORK_DEV, H * V)

    result = lax.map(one_block, (queries.reshape(blocks, FORK_DEV, H * (R + P_SIZE)),
                                 suffix_cache.reshape(blocks, FORK_DEV, R + P_SIZE, S),
                                 owner_slot.reshape(blocks, FORK_DEV),
                                 suffix_len.reshape(blocks, FORK_DEV)))
    return result.reshape(FORKS, H * V)
```

```python
import functools

import jax
import jax.numpy as jnp
from jax import lax
from jax.experimental import pallas as pl
from jax.experimental.pallas import tpu as pltpu
from jax.sharding import Mesh
from jax.sharding import PartitionSpec as P

R = 512
P_SIZE = 64
V = 128
KEY = R + P_SIZE
MOST = 2
COPIES = 4
LANES = 128
SCALE = 192.0 ** (-0.5)
LOG2E = 1.4426950408889634


def row_targets(prompt_col, slot_row, group):
    forks = prompt_col.shape[0]
    prompts = slot_row.shape[1]
    ids = lax.broadcasted_iota(jnp.int32, (forks, prompts), 1)
    owner = jnp.sum(jnp.where(prompt_col == ids, slot_row, 0), axis=1, keepdims=True)
    down = lax.broadcasted_iota(jnp.int32, (forks, forks), 0)
    along = lax.broadcasted_iota(jnp.int32, (forks, forks), 1)

    def turned(column):
        return jnp.sum(jnp.where(down == along, column, 0), axis=0, keepdims=True)

    owner_row = turned(owner)
    before = (owner == owner_row) & (along < down)
    rank = jnp.sum(before.astype(jnp.int32), axis=1, keepdims=True)
    held = COPIES * MOST
    target = (owner % group) * held + (owner // group) * MOST + rank
    return turned(target), target


def place_kernel(group, prompt_ref, slot_ref, q_ref, out_ref):
    target_row, _ = row_targets(prompt_ref[...], slot_ref[...], group)
    rows = out_ref.shape[0]
    at = lax.broadcasted_iota(jnp.int32, (rows, target_row.shape[1]), 0)
    placing = (at == target_row).astype(jnp.bfloat16)
    out_ref[...] = jnp.dot(placing, q_ref[...], preferred_element_type=jnp.float32).astype(
        jnp.bfloat16
    )


def place(prompt, slots, queries, group):
    forks, width = queries.shape
    rows = group * COPIES * MOST
    tile = width // 8
    return pl.pallas_call(
        functools.partial(place_kernel, group),
        out_shape=jax.ShapeDtypeStruct((rows, width), jnp.bfloat16),
        grid=(width // tile,),
        in_specs=[
            pl.BlockSpec(prompt.shape, lambda i: (0, 0)),
            pl.BlockSpec(slots.shape, lambda i: (0, 0)),
            pl.BlockSpec((forks, tile), lambda i: (0, i)),
        ],
        out_specs=pl.BlockSpec((rows, tile), lambda i: (0, i)),
        name="place",
    )(prompt, slots, queries)


def prefix_kernel(group, q_ref, kv_ref, w_ref, out_ref, key_ref, lat_ref, mass_ref):
    step = pl.program_id(0)
    heads = w_ref.shape[0]
    pairs = heads // 2
    quarter = kv_ref.shape[2]

    @pl.when(step == 0)
    def _():
        zero = jnp.zeros((P_SIZE, key_ref.shape[1]), key_ref.dtype)
        key_ref[0:P_SIZE, :] = zero
        key_ref[P_SIZE + KEY : P_SIZE + KEY + P_SIZE, :] = zero

    @pl.when(step % MOST == 0)
    def _():
        for part in range(kv_ref.shape[0]):
            key_ref[P_SIZE : P_SIZE + KEY, part * quarter : (part + 1) * quarter] = kv_ref[part]

    wide = KEY + P_SIZE
    lane = lax.broadcasted_iota(jnp.int32, (group, LANES), 1)
    masses = jnp.zeros((group, LANES), jnp.float32)
    rows = pl.ds(pl.multiple_of(step * group, group), group)
    for odd in range(2):
        query = jnp.concatenate(
            [
                q_ref[:, p * 2 * KEY + odd * R : p * 2 * KEY + odd * R + wide]
                for p in range(pairs)
            ],
            axis=0,
        )
        first = 0 if odd else P_SIZE
        scores = jnp.dot(
            query, key_ref[first : first + wide, :], preferred_element_type=jnp.float32
        )
        peak = jnp.max(scores, axis=1, keepdims=True)
        weights = jnp.exp2((scores - peak) * (SCALE * LOG2E))
        total = jnp.sum(weights, axis=1, keepdims=True)
        summed = lax.dot_general(
            weights.astype(jnp.bfloat16),
            key_ref[P_SIZE : P_SIZE + R, :],
            (((1,), (1,)), ((), ())),
            preferred_element_type=jnp.float32,
        )
        latent = (summed / total).astype(jnp.bfloat16)
        mass = peak * SCALE + jnp.log(total)
        for p in range(pairs):
            head = 2 * p + odd
            lat_ref[head, rows, :] = latent[p * group : (p + 1) * group]
            masses = jnp.where(lane == head, mass[p * group : (p + 1) * group], masses)
    mass_ref[rows, :] = masses

    @pl.when(step == pl.num_programs(0) - 1)
    def _():
        count = mass_ref.shape[0]
        held = count // group
        to = lax.broadcasted_iota(jnp.int32, (count, count), 0)
        come = lax.broadcasted_iota(jnp.int32, (count, count), 1)
        turn = (come == (to % held) * group + to // held).astype(jnp.bfloat16)

        def put(at, block):
            out_ref[:, at : at + block.shape[1]] = jnp.dot(
                turn, block, preferred_element_type=jnp.float32
            ).astype(jnp.bfloat16)

        for head in range(0, heads, 2):
            both = [
                jnp.dot(lat_ref[h], w_ref[h], preferred_element_type=jnp.float32)
                for h in (head, head + 1)
            ]
            put(head * V, jnp.concatenate(both, axis=1).astype(jnp.bfloat16))
        high = mass_ref[...].astype(jnp.bfloat16)
        low = (mass_ref[...] - high.astype(jnp.float32)).astype(jnp.bfloat16)
        put(heads * V, jnp.concatenate([high, low], axis=1))


def prefix(sorted_queries, caches, w_uv, group):
    rows, width = sorted_queries.shape
    heads = w_uv.shape[0]
    steps = rows // group
    parts = caches.shape[0] // COPIES
    length = parts * caches.shape[2]
    return pl.pallas_call(
        functools.partial(prefix_kernel, group),
        out_shape=jax.ShapeDtypeStruct((rows, heads * V + 2 * LANES), jnp.bfloat16),
        grid=(steps,),
        in_specs=[
            pl.BlockSpec((group, width), lambda i: (i, 0)),
            pl.BlockSpec((parts, *caches.shape[1:]), lambda i: (i // MOST, 0, 0)),
            pl.BlockSpec(w_uv.shape, lambda i: (0, 0, 0), pipeline_mode=pl.Buffered(1)),
        ],
        out_specs=pl.BlockSpec((rows, heads * V + 2 * LANES), lambda i: (0, 0)),
        scratch_shapes=[
            pltpu.VMEM((KEY + 2 * P_SIZE, length), jnp.bfloat16),
            pltpu.VMEM((heads, rows, R), jnp.bfloat16),
            pltpu.VMEM((rows, LANES), jnp.float32),
        ],
        compiler_params=pltpu.CompilerParams(vmem_limit_bytes=48 << 20),
        name="prefix",
    )(sorted_queries, caches, w_uv)


def merge_kernel(group, prompt_ref, slot_ref, answer_ref, value_ref, mass_ref, out_ref):
    _, target = row_targets(prompt_ref[...], slot_ref[...], group)
    forks, heads = mass_ref.shape
    rows = answer_ref.shape[0]
    at = lax.broadcasted_iota(jnp.int32, (forks, rows), 1)
    picking = (at == target).astype(jnp.bfloat16)

    def pick(start, size):
        return jnp.dot(
            picking, answer_ref[:, start : start + size], preferred_element_type=jnp.float32
        )

    come = pick(heads * V, 2 * LANES)
    mass_prefix = come[:, :heads] + come[:, LANES : LANES + heads]
    mass_suffix = mass_ref[...]
    top = jnp.maximum(mass_prefix, mass_suffix)
    share_prefix = jnp.exp(mass_prefix - top)
    share_suffix = jnp.exp(mass_suffix - top)
    both = share_prefix + share_suffix
    part_prefix = share_prefix / both
    part_suffix = share_suffix / both
    for head in range(0, heads, 2):
        value = pick(head * V, 2 * V)
        for h in (head, head + 1):
            cut = slice(h * V, (h + 1) * V)
            out_ref[:, cut] = (
                part_prefix[:, h : h + 1] * value[:, (h - head) * V : (h - head + 1) * V]
                + part_suffix[:, h : h + 1] * value_ref[:, cut].astype(jnp.float32)
            ).astype(out_ref.dtype)


def merge(prompt, slots, answer, value_suffix, mass_suffix, group):
    forks = value_suffix.shape[0]
    return pl.pallas_call(
        functools.partial(merge_kernel, group),
        out_shape=jax.ShapeDtypeStruct((forks, value_suffix.shape[1]), jnp.bfloat16),
        compiler_params=pltpu.CompilerParams(vmem_limit_bytes=24 << 20),
        name="merge",
    )(prompt, slots, answer, value_suffix, mass_suffix)


def suffix(queries, suffix_cache, suffix_len, w_uv):
    forks = queries.shape[0]
    heads = w_uv.shape[0]
    query_heads = queries.reshape(forks, heads, KEY)
    scores = (
        jnp.einsum("fhe,fes->fhs", query_heads, suffix_cache, preferred_element_type=jnp.float32)
        * SCALE
    )
    positions = jnp.arange(suffix_cache.shape[2], dtype=jnp.int32)
    live = (positions[None, :] < suffix_len[:, None])[:, None, :]
    scores = jnp.where(live, scores, -jnp.inf)
    peak = jnp.max(scores, axis=2, keepdims=True)
    weights = jnp.where(live, jnp.exp(scores - peak), 0.0)
    total = jnp.sum(weights, axis=2)
    summed = jnp.einsum(
        "fhs,frs->fhr",
        weights.astype(jnp.bfloat16),
        suffix_cache[:, :R, :],
        preferred_element_type=jnp.float32,
    )
    latent = (summed / total[..., None]).astype(jnp.bfloat16)
    value = jnp.einsum("nhr,hrv->nhv", latent, w_uv, preferred_element_type=jnp.float32)
    return value.astype(jnp.bfloat16).reshape(forks, heads * V), peak[..., 0] + jnp.log(total)


def shards(queries, prefix_cache, suffix_cache, w_uv, fork_prompt, prompt_slot, suffix_len):
    near = ("zl", "xc")
    group = lax.axis_size("zl") * lax.axis_size("xc")
    held = COPIES * MOST
    slots = prompt_slot[None, :]
    caches = lax.all_gather(prefix_cache, ("zh", "tp"), axis=0, tiled=True)
    outbound = place(fork_prompt, slots, queries, group)
    width = queries.shape[1]
    received = lax.all_to_all(
        outbound.reshape(group, held, width), near, split_axis=0, concat_axis=0, tiled=True
    )
    by_slot = jnp.swapaxes(received, 0, 1).reshape(held * group, width)
    value_suffix, mass_suffix = suffix(queries, suffix_cache, suffix_len, w_uv)
    by_slot, caches, value_suffix, mass_suffix = lax.optimization_barrier(
        (by_slot, caches, value_suffix, mass_suffix)
    )
    result = prefix(by_slot, caches, w_uv, group)
    answer = lax.all_to_all(
        result.reshape(group, held, result.shape[1]), near, split_axis=0, concat_axis=0, tiled=True
    )
    return merge(
        fork_prompt, slots, answer.reshape(result.shape), value_suffix, mass_suffix, group
    )


def solution(mesh):
    owners = mesh.shape["dp"]
    tp = mesh.shape["tp"]
    group = owners // COPIES
    devices = mesh.devices.reshape(COPIES, 2, group // 2, tp)
    split = Mesh(devices, ("zh", "zl", "xc", "tp"))
    dp = ("zh", "zl", "xc")
    placed = (
        P(dp, "tp"),
        P(dp, None, "tp"),
        P(dp, None, None),
        P("tp", None, None),
        P(dp, None),
        P(),
        P(dp),
    )
    return jax.shard_map(
        shards, mesh=split, in_specs=placed, out_specs=P(dp, "tp"), check_vma=False
    )
```

```python
import jax
import jax.numpy as jnp
from jax import lax
from jax.experimental import pallas as pl
from jax.experimental.pallas import tpu as pltpu
from jax.sharding import Mesh
from jax.sharding import PartitionSpec as P

R = 512
P_SIZE = 64
V = 128
KEY = R + P_SIZE
MOST = 2
COPIES = 4
SPLIT = 4
LANES = 128
SCALE = 192.0 ** (-0.5)
LOG2E = 1.4426950408889634


def row_targets(prompt_col, base_row):
    forks = prompt_col.shape[0]
    prompts = base_row.shape[1]
    ids = lax.broadcasted_iota(jnp.int32, (forks, prompts), 1)
    base = jnp.sum(jnp.where(prompt_col == ids, base_row, 0), axis=1, keepdims=True)
    down = lax.broadcasted_iota(jnp.int32, (forks, forks), 0)
    along = lax.broadcasted_iota(jnp.int32, (forks, forks), 1)

    def turned(column):
        return jnp.sum(jnp.where(down == along, column, 0), axis=0, keepdims=True)

    before = (base == turned(base)) & (along < down)
    target = base + jnp.sum(before.astype(jnp.int32), axis=1, keepdims=True)
    return turned(target), target


def place_kernel(prompt_ref, base_ref, *refs):
    parts = refs[:SPLIT]
    out_ref, placing_ref = refs[SPLIT:]
    forks = parts[0].shape[0]

    @pl.when(pl.program_id(0) == 0)
    def _():
        target_row, _ = row_targets(prompt_ref[...], base_ref[...])
        at = lax.broadcasted_iota(jnp.int32, (out_ref.shape[0], forks), 0)
        for n in range(SPLIT):
            placing_ref[:, n * forks : (n + 1) * forks] = (at == target_row * SPLIT + n).astype(
                jnp.bfloat16
            )

    stacked = jnp.concatenate([part[...] for part in parts], axis=0)
    out_ref[...] = jnp.dot(
        placing_ref[...], stacked, preferred_element_type=jnp.float32
    ).astype(jnp.bfloat16)


def place(prompt, base, queries, group):
    forks, width = queries.shape
    rows = group * COPIES * MOST * SPLIT
    part = width // SPLIT
    steps = 6
    tile = part // steps

    def part_spec(n):
        return pl.BlockSpec((forks, tile), lambda i: (0, n * steps + i))

    return pl.pallas_call(
        place_kernel,
        out_shape=jax.ShapeDtypeStruct((rows, part), jnp.bfloat16),
        grid=(steps,),
        in_specs=[
            pl.BlockSpec(prompt.shape, lambda i: (0, 0)),
            pl.BlockSpec(base.shape, lambda i: (0, 0)),
            *[part_spec(n) for n in range(SPLIT)],
        ],
        out_specs=pl.BlockSpec((rows, tile), lambda i: (0, i)),
        scratch_shapes=[pltpu.VMEM((rows, SPLIT * forks), jnp.bfloat16)],
        name="place",
    )(prompt, base, *[queries] * SPLIT)


def prefix_kernel(
    q_ref, kv_ref, w_hbm, out_ref, w_ref, key_ref, lat_ref, part_ref, cell_ref, mass_ref, sem
):
    step = pl.program_id(0)
    last = pl.num_programs(0) - 1
    heads = w_ref.shape[0]
    group = q_ref.shape[0]
    held = COPIES * MOST
    quarter = kv_ref.shape[2]
    fetch = pltpu.make_async_copy(w_hbm, w_ref, sem)

    @pl.when(step == 0)
    def _():
        fetch.start()
        zero = jnp.zeros((P_SIZE, key_ref.shape[1]), key_ref.dtype)
        key_ref[0:P_SIZE, :] = zero
        key_ref[P_SIZE + KEY : P_SIZE + KEY + P_SIZE, :] = zero

    for n in range(kv_ref.shape[0]):
        key_ref[P_SIZE : P_SIZE + KEY, n * quarter : (n + 1) * quarter] = kv_ref[n]

    wide = KEY + P_SIZE
    tall = group * MOST * SPLIT
    span = group * MOST
    pairs = heads // SPLIT // 2
    lane = lax.broadcasted_iota(jnp.int32, (tall, LANES), 1)
    cells = jnp.zeros((tall, LANES), jnp.float32)
    rows = pl.ds(pl.multiple_of(step * span, span), span)

    def score(odd):
        query = jnp.concatenate(
            [
                q_ref[:, :, p * 2 * KEY + odd * R : p * 2 * KEY + odd * R + wide].reshape(
                    tall, wide
                )
                for p in range(pairs)
            ],
            axis=0,
        )
        first = 0 if odd else P_SIZE
        return jnp.dot(query, key_ref[first : first + wide, :], preferred_element_type=jnp.float32)

    ahead = [score(0), score(1)]
    for odd in range(2):
        scores = ahead[odd]
        peak = jnp.max(scores, axis=1, keepdims=True)
        weights = jnp.exp2((scores - peak) * (SCALE * LOG2E))
        total = jnp.sum(weights, axis=1, keepdims=True)
        summed = lax.dot_general(
            weights.astype(jnp.bfloat16),
            key_ref[P_SIZE : P_SIZE + R, :],
            (((1,), (1,)), ((), ())),
            preferred_element_type=jnp.float32,
        )
        latent = summed / total
        for b in range(R // LANES):
            part_ref[b] = latent[:, b * LANES : (b + 1) * LANES]
        mass = peak * SCALE + jnp.log(total)
        for p in range(pairs):
            cells = jnp.where(lane == 2 * p + odd, mass[p * tall : (p + 1) * tall], cells)
            for n in range(SPLIT):
                head = n * 2 * pairs + 2 * p + odd
                for b in range(R // LANES):
                    lat_ref[head, rows, b * LANES : (b + 1) * LANES] = part_ref[
                        b, pl.ds(p * tall + n, span, stride=SPLIT), :
                    ].astype(jnp.bfloat16)
    cell_ref[...] = cells
    masses = jnp.zeros((span, LANES), jnp.float32)
    for n in range(SPLIT):
        block = cell_ref[pl.ds(n, span, stride=SPLIT), :]
        masses = masses + (pltpu.roll(block, n * 2 * pairs, 1) if n else block)
    mass_ref[rows, :] = masses

    @pl.when(step == last)
    def _():
        fetch.wait()
        count = mass_ref.shape[0]
        to = lax.broadcasted_iota(jnp.int32, (count, count), 0)
        come = lax.broadcasted_iota(jnp.int32, (count, count), 1)
        source, slot = to // held, to % held
        turn = (come == (slot // MOST) * span + source * MOST + slot % MOST).astype(jnp.bfloat16)

        def put(at, block):
            out_ref[:, at : at + block.shape[1]] = jnp.dot(
                turn, block, preferred_element_type=jnp.float32
            ).astype(jnp.bfloat16)

        for head in range(0, heads, 2):
            both = [
                jnp.dot(lat_ref[h], w_ref[h], preferred_element_type=jnp.float32)
                for h in (head, head + 1)
            ]
            put(head * V, jnp.concatenate(both, axis=1).astype(jnp.bfloat16))
        high = mass_ref[...].astype(jnp.bfloat16)
        low = (mass_ref[...] - high.astype(jnp.float32)).astype(jnp.bfloat16)
        put(heads * V, jnp.concatenate([high, low], axis=1))


def prefix(received, caches, w_uv):
    group, _, part = received.shape
    heads = w_uv.shape[0]
    rows = group * COPIES * MOST
    tall = group * MOST * SPLIT
    parts = caches.shape[0] // COPIES
    length = parts * caches.shape[2]
    caches = caches.reshape(parts, COPIES, *caches.shape[1:])
    wide = heads * V + 2 * LANES
    return pl.pallas_call(
        prefix_kernel,
        out_shape=jax.ShapeDtypeStruct((rows, wide), jnp.bfloat16),
        grid=(COPIES,),
        in_specs=[
            pl.BlockSpec((group, MOST * SPLIT, part), lambda i: (0, i, 0)),
            pl.BlockSpec((parts, None, *caches.shape[2:]), lambda i: (0, i, 0, 0)),
            pl.BlockSpec(memory_space=pl.ANY),
        ],
        out_specs=pl.BlockSpec((rows, wide), lambda i: (0, 0)),
        scratch_shapes=[
            pltpu.VMEM(w_uv.shape, jnp.bfloat16),
            pltpu.VMEM((KEY + 2 * P_SIZE, length), jnp.bfloat16),
            pltpu.VMEM((heads, rows, R), jnp.bfloat16),
            pltpu.VMEM((R // LANES, heads // SPLIT // 2 * tall, LANES), jnp.float32),
            pltpu.VMEM((tall, LANES), jnp.float32),
            pltpu.VMEM((rows, LANES), jnp.float32),
            pltpu.SemaphoreType.DMA,
        ],
        compiler_params=pltpu.CompilerParams(vmem_limit_bytes=52 << 20),
        name="prefix",
    )(received, caches, w_uv)


def merge_kernel(prompt_ref, base_ref, answer_ref, value_ref, mass_ref, out_ref):
    _, target = row_targets(prompt_ref[...], base_ref[...])
    forks, heads = mass_ref.shape
    rows = answer_ref.shape[0]
    at = lax.broadcasted_iota(jnp.int32, (forks, rows), 1)
    picking = (at == target).astype(jnp.bfloat16)

    def pick(start, size):
        return jnp.dot(
            picking, answer_ref[:, start : start + size], preferred_element_type=jnp.float32
        )

    come = pick(heads * V, 2 * LANES)
    mass_prefix = come[:, :heads] + come[:, LANES : LANES + heads]
    mass_suffix = mass_ref[...]
    top = jnp.maximum(mass_prefix, mass_suffix)
    share_prefix = jnp.exp(mass_prefix - top)
    share_suffix = jnp.exp(mass_suffix - top)
    both = share_prefix + share_suffix
    part_prefix = share_prefix / both
    part_suffix = share_suffix / both
    for head in range(0, heads, 2):
        value = pick(head * V, 2 * V)
        for h in (head, head + 1):
            cut = slice(h * V, (h + 1) * V)
            out_ref[:, cut] = (
                part_prefix[:, h : h + 1] * value[:, (h - head) * V : (h - head + 1) * V]
                + part_suffix[:, h : h + 1] * value_ref[:, cut].astype(jnp.float32)
            ).astype(out_ref.dtype)


def merge(prompt, base, answer, value_suffix, mass_suffix):
    forks = value_suffix.shape[0]
    return pl.pallas_call(
        merge_kernel,
        out_shape=jax.ShapeDtypeStruct((forks, value_suffix.shape[1]), jnp.bfloat16),
        compiler_params=pltpu.CompilerParams(vmem_limit_bytes=24 << 20),
        name="merge",
    )(prompt, base, answer, value_suffix, mass_suffix)


def suffix(queries, suffix_cache, suffix_len, w_uv):
    forks = queries.shape[0]
    heads = w_uv.shape[0]
    query_heads = queries.reshape(forks, heads, KEY)
    scores = (
        jnp.einsum("fhe,fes->fhs", query_heads, suffix_cache, preferred_element_type=jnp.float32)
        * SCALE
    )
    positions = jnp.arange(suffix_cache.shape[2], dtype=jnp.int32)
    live = (positions[None, :] < suffix_len[:, None])[:, None, :]
    scores = jnp.where(live, scores, -jnp.inf)
    peak = jnp.max(scores, axis=2, keepdims=True)
    weights = jnp.where(live, jnp.exp(scores - peak), 0.0)
    total = jnp.sum(weights, axis=2)
    summed = jnp.einsum(
        "fhs,frs->fhr",
        weights.astype(jnp.bfloat16),
        suffix_cache[:, :R, :],
        preferred_element_type=jnp.float32,
    )
    latent = (summed / total[..., None]).astype(jnp.bfloat16)
    value = jnp.einsum("nhr,hrv->nhv", latent, w_uv, preferred_element_type=jnp.float32)
    return value.astype(jnp.bfloat16).reshape(forks, heads * V), peak[..., 0] + jnp.log(total)


def shards(queries, prefix_cache, suffix_cache, w_uv, fork_prompt, prompt_slot, suffix_len):
    near = ("zl", "xc")
    group = lax.axis_size("zl") * lax.axis_size("xc")
    held = COPIES * MOST
    back = (lax.axis_index("zh") - prompt_slot // group) % COPIES
    base = ((prompt_slot % group) * held + back * MOST)[None, :].astype(jnp.int32)

    def from_behind(steps):
        return lax.ppermute(
            prefix_cache, "zh", [(n, (n + steps) % COPIES) for n in range(COPIES)]
        )

    moved = [from_behind(1), from_behind(3), from_behind(2)]
    outbound = place(fork_prompt, base, queries, group)
    outbound, *moved = lax.optimization_barrier((outbound, *moved))
    stacked = jnp.concatenate([prefix_cache, moved[0], moved[2], moved[1]], axis=0)
    caches = lax.all_gather(stacked, "tp", axis=0, tiled=True)
    received = lax.all_to_all(
        outbound.reshape(group, held * SPLIT, queries.shape[1] // SPLIT),
        near,
        split_axis=0,
        concat_axis=0,
        tiled=True,
    )
    value_suffix, mass_suffix = suffix(queries, suffix_cache, suffix_len, w_uv)
    received, caches, value_suffix, mass_suffix = lax.optimization_barrier(
        (received, caches, value_suffix, mass_suffix)
    )
    result = prefix(received, caches, w_uv)
    answer = lax.all_to_all(
        result.reshape(group, held, result.shape[1]), near, split_axis=0, concat_axis=0, tiled=True
    )
    return merge(fork_prompt, base, answer.reshape(result.shape), value_suffix, mass_suffix)


def solution(mesh):
    owners = mesh.shape["dp"]
    tp = mesh.shape["tp"]
    group = owners // COPIES
    devices = mesh.devices.reshape(COPIES, 2, group // 2, tp)
    split = Mesh(devices, ("zh", "zl", "xc", "tp"))
    dp = ("zh", "zl", "xc")
    placed = (
        P(dp, "tp"),
        P(dp, None, "tp"),
        P(dp, None, None),
        P("tp", None, None),
        P(dp, None),
        P(),
        P(dp),
    )
    return jax.shard_map(
        shards, mesh=split, in_specs=placed, out_specs=P(dp, "tp"), check_vma=False
    )
```

```python
import functools

import jax
import jax.numpy as jnp
from jax import lax
from jax.experimental import pallas as pl
from jax.experimental.pallas import tpu as pltpu
from jax.sharding import Mesh
from jax.sharding import PartitionSpec as P

R = 512
P_SIZE = 64
V = 128
KEY = R + P_SIZE
MOST = 2
COPIES = 4
SPLIT = 4
HALVES = 2
CHUNKS = 2
LANES = 128
SCALE = 192.0 ** (-0.5)
LOG2E = 1.4426950408889634


def row_targets(prompt_col, base_row):
    forks = prompt_col.shape[0]
    prompts = base_row.shape[1]
    ids = lax.broadcasted_iota(jnp.int32, (forks, prompts), 1)
    base = jnp.sum(jnp.where(prompt_col == ids, base_row, 0), axis=1, keepdims=True)
    down = lax.broadcasted_iota(jnp.int32, (forks, forks), 0)
    along = lax.broadcasted_iota(jnp.int32, (forks, forks), 1)

    def turned(column):
        return jnp.sum(jnp.where(down == along, column, 0), axis=0, keepdims=True)

    before = (base == turned(base)) & (along < down)
    target = base + jnp.sum(before.astype(jnp.int32), axis=1, keepdims=True)
    return turned(target), target


def place_kernel(prompt_ref, base_ref, *refs):
    parts = refs[:SPLIT]
    out_ref, placing_ref = refs[SPLIT:]
    forks = parts[0].shape[0]

    @pl.when(pl.program_id(0) == 0)
    def _():
        target_row, _ = row_targets(prompt_ref[...], base_ref[...])
        at = lax.broadcasted_iota(jnp.int32, (out_ref.shape[0], forks), 0)
        for n in range(SPLIT):
            placing_ref[:, n * forks : (n + 1) * forks] = (at == target_row * SPLIT + n).astype(
                jnp.bfloat16
            )

    def paired(part):
        odd = part[:, KEY:]
        return jnp.concatenate([part[:, :R], odd[:, :R], part[:, R:KEY], odd[:, R:]], axis=1)

    stacked = jnp.concatenate([paired(part[...]) for part in parts], axis=0)
    out_ref[...] = jnp.dot(
        placing_ref[...], stacked, preferred_element_type=jnp.float32
    ).astype(jnp.bfloat16)


def place(prompt, base, queries, group, half):
    forks, width = queries.shape
    rows = group * COPIES * MOST * SPLIT
    part = width // SPLIT
    tile = 2 * KEY
    steps = part // tile
    mine = steps // HALVES

    def part_spec(n):
        return pl.BlockSpec((forks, tile), lambda i: (0, n * steps + half * mine + i))

    return pl.pallas_call(
        place_kernel,
        out_shape=jax.ShapeDtypeStruct((rows, part // HALVES), jnp.bfloat16),
        grid=(mine,),
        in_specs=[
            pl.BlockSpec(prompt.shape, lambda i: (0, 0)),
            pl.BlockSpec(base.shape, lambda i: (0, 0)),
            *[part_spec(n) for n in range(SPLIT)],
        ],
        out_specs=pl.BlockSpec((rows, tile), lambda i: (0, i)),
        scratch_shapes=[pltpu.VMEM((rows, SPLIT * forks), jnp.bfloat16)],
        name="place",
    )(prompt, base, *[queries] * SPLIT)


def prefix_kernel(
    half, q_ref, kv_ref, w_hbm, out_ref, w_ref, key_ref, lat_ref, part_ref, cell_ref, mass_ref, sem
):
    step = pl.program_id(0)
    last = pl.num_programs(0) - 1
    heads = w_ref.shape[0]
    group = q_ref.shape[0]
    held = COPIES * MOST
    quarter = kv_ref.shape[2]
    run = heads // SPLIT
    fetches = [
        pltpu.make_async_copy(
            w_hbm.at[pl.ds((n * HALVES + half) * run, run)],
            w_ref.at[pl.ds(n * run, run)],
            sem.at[n],
        )
        for n in range(SPLIT)
    ]

    @pl.when(step == 0)
    def _():
        for fetch in fetches:
            fetch.start()

    for n in range(kv_ref.shape[0]):
        cut = slice(n * quarter, (n + 1) * quarter)
        key_ref[0:KEY, cut] = kv_ref[n]
        key_ref[KEY : KEY + P_SIZE, cut] = kv_ref[n, R:KEY, :]

    tall = group * MOST * SPLIT
    span = group * MOST
    pairs = heads // SPLIT // 2
    lane = lax.broadcasted_iota(jnp.int32, (tall, LANES), 1)
    cells = jnp.zeros((tall, LANES), jnp.float32)
    rows = pl.ds(pl.multiple_of(step * span, span), span)

    def piece(start, size):
        return q_ref[:, :, start : start + size].reshape(tall, size)

    def query(pair, odd):
        start = pair * 2 * KEY
        ropes = piece(start + 2 * R, LANES)
        mine = (lane >= P_SIZE) if odd else (lane < P_SIZE)
        return jnp.concatenate(
            [piece(start + odd * R, R), jnp.where(mine, ropes, jnp.zeros_like(ropes))], axis=1
        )

    order = [(pair, odd) for odd in range(2) for pair in range(pairs)]
    chunks = CHUNKS
    per = len(order) // chunks

    def score(chunk):
        return jnp.dot(
            jnp.concatenate([query(*one) for one in order[chunk * per : (chunk + 1) * per]], axis=0),
            key_ref[...],
            preferred_element_type=jnp.float32,
        )

    ahead = [score(chunk) for chunk in range(1)]
    for chunk in range(chunks):
        scores = ahead.pop(0)
        if chunk + 1 < chunks:
            ahead.append(score(chunk + 1))
        peak = jnp.max(scores, axis=1, keepdims=True)
        weights = jnp.exp2((scores - peak) * (SCALE * LOG2E))
        total = jnp.sum(weights, axis=1, keepdims=True)
        summed = lax.dot_general(
            weights.astype(jnp.bfloat16),
            key_ref[0:R, :],
            (((1,), (1,)), ((), ())),
            preferred_element_type=jnp.float32,
        )
        latent = summed * (1.0 / total)
        for b in range(R // LANES):
            part_ref[b, chunk * per * tall : (chunk + 1) * per * tall, :] = latent[:, b * LANES : (b + 1) * LANES]
        mass = peak * SCALE + jnp.log(total)
        for at, (pair, odd) in enumerate(order[chunk * per : (chunk + 1) * per]):
            cells = jnp.where(lane == 2 * pair + odd, mass[at * tall : (at + 1) * tall], cells)
    for at, (pair, odd) in enumerate(order):
        for n in range(SPLIT):
            head = n * 2 * pairs + 2 * pair + odd
            for b in range(R // LANES):
                lat_ref[head, rows, b * LANES : (b + 1) * LANES] = part_ref[
                    b, pl.ds(at * tall + n, span, stride=SPLIT), :
                ].astype(jnp.bfloat16)
    cell_ref[...] = cells
    masses = jnp.zeros((span, LANES), jnp.float32)
    for n in range(SPLIT):
        block = cell_ref[pl.ds(n, span, stride=SPLIT), :]
        masses = masses + (pltpu.roll(block, n * 2 * pairs, 1) if n else block)
    mass_ref[rows, :] = masses

    @pl.when(step == last)
    def _():
        for fetch in fetches:
            fetch.wait()
        count = mass_ref.shape[0]
        to = lax.broadcasted_iota(jnp.int32, (count, count), 0)
        come = lax.broadcasted_iota(jnp.int32, (count, count), 1)
        source, slot = to // held, to % held
        turn = (come == (slot // MOST) * span + source * MOST + slot % MOST).astype(jnp.bfloat16)

        def put(at, block):
            out_ref[:, at : at + block.shape[1]] = jnp.dot(
                turn, block, preferred_element_type=jnp.float32
            ).astype(jnp.bfloat16)

        for head in range(0, heads, 2):
            both = [
                jnp.dot(lat_ref[h], w_ref[h], preferred_element_type=jnp.float32)
                for h in (head, head + 1)
            ]
            put(head * V, jnp.concatenate(both, axis=1).astype(jnp.bfloat16))
        high = mass_ref[...].astype(jnp.bfloat16)
        low = (mass_ref[...] - high.astype(jnp.float32)).astype(jnp.bfloat16)
        put(heads * V, jnp.concatenate([high, low], axis=1))


def prefix(received, caches, w_uv, half):
    group, _, part = received.shape
    heads = w_uv.shape[0] // HALVES
    rows = group * COPIES * MOST
    tall = group * MOST * SPLIT
    parts = caches.shape[0] // COPIES
    length = parts * caches.shape[2]
    caches = caches.reshape(parts, COPIES, *caches.shape[1:])
    wide = heads * V + 2 * LANES
    return pl.pallas_call(
        functools.partial(prefix_kernel, half),
        out_shape=jax.ShapeDtypeStruct((rows, wide), jnp.bfloat16),
        grid=(COPIES,),
        in_specs=[
            pl.BlockSpec((group, MOST * SPLIT, part), lambda i: (0, i, 0)),
            pl.BlockSpec((parts, None, *caches.shape[2:]), lambda i: (0, i, 0, 0)),
            pl.BlockSpec(memory_space=pl.ANY),
        ],
        out_specs=pl.BlockSpec((rows, wide), lambda i: (0, 0)),
        scratch_shapes=[
            pltpu.VMEM((heads, *w_uv.shape[1:]), jnp.bfloat16),
            pltpu.VMEM((KEY + P_SIZE, length), jnp.bfloat16),
            pltpu.VMEM((heads, rows, R), jnp.bfloat16),
            pltpu.VMEM((R // LANES, heads // SPLIT * tall, LANES), jnp.float32),
            pltpu.VMEM((tall, LANES), jnp.float32),
            pltpu.VMEM((rows, LANES), jnp.float32),
            pltpu.SemaphoreType.DMA((SPLIT,)),
        ],
        compiler_params=pltpu.CompilerParams(vmem_limit_bytes=56 << 20),
        cost_estimate=pl.CostEstimate(
            flops=2 * rows * heads * length * (KEY + R) + 2 * rows * heads * R * V,
            bytes_accessed=2 * (received.size + caches.size + w_uv.size // HALVES + rows * wide),
            transcendentals=rows * heads * length,
        ),
        name="prefix",
    )(received, caches, w_uv)


def merge_kernel(prompt_ref, base_ref, *refs):
    answers = refs[:HALVES]
    value_ref, mass_ref, out_ref = refs[HALVES:]
    _, target = row_targets(prompt_ref[...], base_ref[...])
    forks, heads = mass_ref.shape
    run = heads // SPLIT // HALVES
    at = lax.broadcasted_iota(jnp.int32, (forks, answers[0].shape[0]), 1)
    picking = (at == target).astype(jnp.bfloat16)

    def pick(ref, start, size):
        return jnp.dot(
            picking, ref[:, start : start + size], preferred_element_type=jnp.float32
        )

    for half, answer in enumerate(answers):
        come = pick(answer, heads // HALVES * V, 2 * LANES)
        mass = come[:, :LANES] + come[:, LANES:]
        for n in range(SPLIT):
            first = (n * HALVES + half) * run
            mass_prefix = mass[:, n * run : (n + 1) * run]
            mass_suffix = mass_ref[:, first : first + run]
            top = jnp.maximum(mass_prefix, mass_suffix)
            share_prefix = jnp.exp(mass_prefix - top)
            share_suffix = jnp.exp(mass_suffix - top)
            both = share_prefix + share_suffix
            part_prefix = share_prefix / both
            part_suffix = share_suffix / both
            value = pick(answer, n * run * V, run * V)
            for h in range(run):
                cut = slice((first + h) * V, (first + h + 1) * V)
                out_ref[:, cut] = (
                    part_prefix[:, h : h + 1] * value[:, h * V : (h + 1) * V]
                    + part_suffix[:, h : h + 1] * value_ref[:, cut].astype(jnp.float32)
                ).astype(out_ref.dtype)


def merge(prompt, base, answers, value_suffix, mass_suffix):
    forks = value_suffix.shape[0]
    return pl.pallas_call(
        merge_kernel,
        out_shape=jax.ShapeDtypeStruct((forks, value_suffix.shape[1]), jnp.bfloat16),
        compiler_params=pltpu.CompilerParams(vmem_limit_bytes=24 << 20),
        name="merge",
    )(prompt, base, *answers, value_suffix, mass_suffix)


def suffix(queries, suffix_cache, suffix_len, w_uv):
    forks = queries.shape[0]
    heads = w_uv.shape[0]
    query_heads = queries.reshape(forks, heads, KEY)
    scores = (
        jnp.einsum("fhe,fes->fhs", query_heads, suffix_cache, preferred_element_type=jnp.float32)
        * SCALE
    )
    positions = jnp.arange(suffix_cache.shape[2], dtype=jnp.int32)
    live = (positions[None, :] < suffix_len[:, None])[:, None, :]
    scores = jnp.where(live, scores, -jnp.inf)
    peak = jnp.max(scores, axis=2, keepdims=True)
    weights = jnp.where(live, jnp.exp(scores - peak), 0.0)
    total = jnp.sum(weights, axis=2)
    summed = jnp.einsum(
        "fhs,frs->fhr",
        weights.astype(jnp.bfloat16),
        suffix_cache[:, :R, :],
        preferred_element_type=jnp.float32,
    )
    latent = (summed / total[..., None]).astype(jnp.bfloat16)
    value = jnp.einsum("nhr,hrv->nhv", latent, w_uv, preferred_element_type=jnp.float32)
    return value.astype(jnp.bfloat16).reshape(forks, heads * V), peak[..., 0] + jnp.log(total)


def shards(queries, prefix_cache, suffix_cache, w_uv, fork_prompt, prompt_slot, suffix_len):
    near = ("zl", "xc")
    group = lax.axis_size("zl") * lax.axis_size("xc")
    held = COPIES * MOST
    back = (lax.axis_index("zh") - prompt_slot // group) % COPIES
    base = ((prompt_slot % group) * held + back * MOST)[None, :].astype(jnp.int32)

    def from_behind(steps):
        return lax.ppermute(
            prefix_cache, "zh", [(n, (n + steps) % COPIES) for n in range(COPIES)]
        )

    def exchange(value):
        return lax.all_to_all(
            value.reshape(group, -1, value.shape[1]), near, split_axis=0, concat_axis=0, tiled=True
        )

    moved = [from_behind(n) for n in range(1, COPIES)]
    outbound = [place(fork_prompt, base, queries, group, half) for half in range(HALVES)]
    outbound[0], *moved = lax.optimization_barrier((outbound[0], *moved))
    caches = lax.all_gather(
        jnp.concatenate([prefix_cache, *moved], axis=0), "tp", axis=0, tiled=True
    )
    value_suffix, mass_suffix = suffix(queries, suffix_cache, suffix_len, w_uv)
    received = [exchange(outbound[0])]
    outbound[1], value_suffix, mass_suffix = lax.optimization_barrier(
        (outbound[1], value_suffix, mass_suffix)
    )
    received.append(exchange(outbound[1]))
    results = [prefix(received[0], caches, w_uv, 0)]
    received[1], results[0] = lax.optimization_barrier((received[1], results[0]))
    results.append(prefix(received[1], caches, w_uv, 1))
    answers = [exchange(result) for result in results]
    answers = [answer.reshape(-1, answer.shape[2]) for answer in answers]
    return merge(fork_prompt, base, answers, value_suffix, mass_suffix)


def solution(mesh):
    owners = mesh.shape["dp"]
    tp = mesh.shape["tp"]
    group = owners // COPIES
    devices = mesh.devices.reshape(COPIES, 2, group // 2, tp)
    split = Mesh(devices, ("zh", "zl", "xc", "tp"))
    dp = ("zh", "zl", "xc")
    placed = (
        P(dp, "tp"),
        P(dp, None, "tp"),
        P(dp, None, None),
        P("tp", None, None),
        P(dp, None),
        P(),
        P(dp),
    )
    return jax.shard_map(
        shards, mesh=split, in_specs=placed, out_specs=P(dp, "tp"), check_vma=False
    )
```

```python
import functools

import jax
import jax.numpy as jnp
from jax import lax
from jax.experimental import pallas as pl
from jax.experimental.pallas import tpu as pltpu
from jax.sharding import Mesh
from jax.sharding import PartitionSpec as P

R = 512
P_SIZE = 64
V = 128
KEY = R + P_SIZE
MOST = 2
COPIES = 4
SPLIT = 4
PARTS = ((0, 3), (3, 1))
CHUNKS = 2
LANES = 128
SCALE = 192.0 ** (-0.5)
LOG2E = 1.4426950408889634


def row_targets(prompt_col, base_row):
    forks = prompt_col.shape[0]
    prompts = base_row.shape[1]
    ids = lax.broadcasted_iota(jnp.int32, (forks, prompts), 1)
    base = jnp.sum(jnp.where(prompt_col == ids, base_row, 0), axis=1, keepdims=True)
    down = lax.broadcasted_iota(jnp.int32, (forks, forks), 0)
    along = lax.broadcasted_iota(jnp.int32, (forks, forks), 1)

    def turned(column):
        return jnp.sum(jnp.where(down == along, column, 0), axis=0, keepdims=True)

    before = (base == turned(base)) & (along < down)
    target = base + jnp.sum(before.astype(jnp.int32), axis=1, keepdims=True)
    return turned(target), target


def place_kernel(prompt_ref, base_ref, *refs):
    parts = refs[:SPLIT]
    out_ref, target_ref, placing_ref = refs[SPLIT:]
    forks = parts[0].shape[0]

    @pl.when(pl.program_id(0) == 0)
    def _():
        target_row, target_ref[...] = row_targets(prompt_ref[...], base_ref[...])
        at = lax.broadcasted_iota(jnp.int32, (out_ref.shape[0], forks), 0)
        for n in range(SPLIT):
            placing_ref[:, n * forks : (n + 1) * forks] = (at == target_row * SPLIT + n).astype(
                jnp.bfloat16
            )

    def paired(part):
        odd = part[:, KEY:]
        return jnp.concatenate([part[:, :R], odd[:, :R], part[:, R:KEY], odd[:, R:]], axis=1)

    stacked = jnp.concatenate([paired(part[...]) for part in parts], axis=0)
    out_ref[...] = jnp.dot(
        placing_ref[...], stacked, preferred_element_type=jnp.float32
    ).astype(jnp.bfloat16)


def place(prompt, base, queries, group, part):
    forks, width = queries.shape
    rows = group * COPIES * MOST * SPLIT
    tile = 2 * KEY
    steps = width // SPLIT // tile
    first, mine = part

    def part_spec(n):
        return pl.BlockSpec((forks, tile), lambda i: (0, n * steps + first + i))

    return pl.pallas_call(
        place_kernel,
        out_shape=(
            jax.ShapeDtypeStruct((rows, mine * tile), jnp.bfloat16),
            jax.ShapeDtypeStruct((forks, 1), jnp.int32),
        ),
        grid=(mine,),
        in_specs=[
            pl.BlockSpec(prompt.shape, lambda i: (0, 0)),
            pl.BlockSpec(base.shape, lambda i: (0, 0)),
            *[part_spec(n) for n in range(SPLIT)],
        ],
        out_specs=(
            pl.BlockSpec((rows, tile), lambda i: (0, i)),
            pl.BlockSpec((forks, 1), lambda i: (0, 0)),
        ),
        scratch_shapes=[pltpu.VMEM((rows, SPLIT * forks), jnp.bfloat16)],
        name="place",
    )(prompt, base, *[queries] * SPLIT)


def prefix_kernel(part, q_ref, own_ref, kv_ref, w_hbm, *refs):
    *earlier, out_ref, w_ref, key_ref, lat_ref, part_ref, cell_ref, mass_ref, sem = refs
    ahead_of_it = earlier[0].shape[1] if earlier else 0
    step = pl.program_id(0)
    last = pl.num_programs(0) - 1
    heads = w_ref.shape[0]
    group = q_ref.shape[0]
    held = COPIES * MOST
    quarter = kv_ref.shape[2]
    run = heads // SPLIT
    group_heads = w_hbm.shape[0] // SPLIT
    fetches = [
        pltpu.make_async_copy(
            w_hbm.at[pl.ds(n * group_heads + 2 * part[0], run)],
            w_ref.at[pl.ds(n * run, run)],
            sem.at[n],
        )
        for n in range(SPLIT)
    ]

    @pl.when(step == 0)
    def _():
        for fetch in fetches:
            fetch.start()
        if earlier:
            out_ref[:, :ahead_of_it] = earlier[0][...]

    def keep(ref):
        for n in range(ref.shape[0]):
            cut = slice(n * quarter, (n + 1) * quarter)
            key_ref[0:KEY, cut] = ref[n]
            key_ref[KEY : KEY + P_SIZE, cut] = ref[n, R:KEY, :]

    @pl.when(step == 0)
    def _():
        keep(own_ref)

    @pl.when(step > 0)
    def _():
        keep(kv_ref)

    tall = group * MOST * SPLIT
    span = group * MOST
    pairs = heads // SPLIT // 2
    lane = lax.broadcasted_iota(jnp.int32, (tall, LANES), 1)
    cells = jnp.zeros((tall, LANES), jnp.float32)
    rows = pl.ds(pl.multiple_of(step * span, span), span)

    def piece(start, size):
        return q_ref[:, :, start : start + size].reshape(tall, size)

    def query(pair, odd):
        start = pair * 2 * KEY
        ropes = piece(start + 2 * R, LANES)
        mine = (lane >= P_SIZE) if odd else (lane < P_SIZE)
        return jnp.concatenate(
            [piece(start + odd * R, R), jnp.where(mine, ropes, jnp.zeros_like(ropes))], axis=1
        )

    order = [(pair, odd) for odd in range(2) for pair in range(pairs)]
    chunks = CHUNKS if len(order) > CHUNKS else 1
    per = len(order) // chunks

    def score(chunk):
        return jnp.dot(
            jnp.concatenate([query(*one) for one in order[chunk * per : (chunk + 1) * per]], axis=0),
            key_ref[...],
            preferred_element_type=jnp.float32,
        )

    ahead = [score(chunk) for chunk in range(1)]
    for chunk in range(chunks):
        scores = ahead.pop(0)
        if chunk + 1 < chunks:
            ahead.append(score(chunk + 1))
        peak = jnp.max(scores, axis=1, keepdims=True)
        weights = jnp.exp2((scores - peak) * (SCALE * LOG2E))
        total = jnp.sum(weights, axis=1, keepdims=True)
        summed = lax.dot_general(
            weights.astype(jnp.bfloat16),
            key_ref[0:R, :],
            (((1,), (1,)), ((), ())),
            preferred_element_type=jnp.float32,
        )
        latent = summed * (1.0 / total)
        for b in range(R // LANES):
            part_ref[b, chunk * per * tall : (chunk + 1) * per * tall, :] = latent[:, b * LANES : (b + 1) * LANES]
        mass = peak * SCALE + jnp.log(total)
        for at, (pair, odd) in enumerate(order[chunk * per : (chunk + 1) * per]):
            cells = jnp.where(lane == 2 * pair + odd, mass[at * tall : (at + 1) * tall], cells)
    for at, (pair, odd) in enumerate(order):
        for n in range(SPLIT):
            head = n * 2 * pairs + 2 * pair + odd
            for b in range(R // LANES):
                lat_ref[head, rows, b * LANES : (b + 1) * LANES] = part_ref[
                    b, pl.ds(at * tall + n, span, stride=SPLIT), :
                ].astype(jnp.bfloat16)
    cell_ref[...] = cells
    masses = jnp.zeros((span, LANES), jnp.float32)
    for n in range(SPLIT):
        block = cell_ref[pl.ds(n, span, stride=SPLIT), :]
        masses = masses + (pltpu.roll(block, n * 2 * pairs, 1) if n else block)
    mass_ref[rows, :] = masses

    @pl.when(step == last)
    def _():
        for fetch in fetches:
            fetch.wait()
        count = mass_ref.shape[0]
        to = lax.broadcasted_iota(jnp.int32, (count, count), 0)
        come = lax.broadcasted_iota(jnp.int32, (count, count), 1)
        source, slot = to // held, to % held
        turn = (come == (slot // MOST) * span + source * MOST + slot % MOST).astype(jnp.bfloat16)

        def put(at, block):
            begin = ahead_of_it + at
            out_ref[:, begin : begin + block.shape[1]] = jnp.dot(
                turn, block, preferred_element_type=jnp.float32
            ).astype(jnp.bfloat16)

        for head in range(0, heads, 2):
            both = [
                jnp.dot(lat_ref[h], w_ref[h], preferred_element_type=jnp.float32)
                for h in (head, head + 1)
            ]
            put(head * V, jnp.concatenate(both, axis=1).astype(jnp.bfloat16))
        high = mass_ref[...].astype(jnp.bfloat16)
        low = (mass_ref[...] - high.astype(jnp.float32)).astype(jnp.bfloat16)
        put(heads * V, jnp.concatenate([high, low], axis=1))


def prefix(received, own, caches, w_uv, part, *earlier):
    group, _, width = received.shape
    heads = 2 * part[1] * SPLIT
    rows = group * COPIES * MOST
    tall = group * MOST * SPLIT
    parts = own.shape[0]
    length = parts * own.shape[2]
    wide = heads * V + 2 * LANES + sum(one.shape[1] for one in earlier)
    return pl.pallas_call(
        functools.partial(prefix_kernel, part),
        out_shape=jax.ShapeDtypeStruct((rows, wide), jnp.bfloat16),
        grid=(COPIES,),
        in_specs=[
            pl.BlockSpec((group, MOST * SPLIT, width), lambda i: (0, i, 0)),
            pl.BlockSpec(own.shape, lambda i: (0, 0, 0), pipeline_mode=pl.Buffered(1)),
            pl.BlockSpec(
                (parts, None, *caches.shape[2:]), lambda i: (0, jnp.maximum(i - 1, 0), 0, 0)
            ),
            pl.BlockSpec(memory_space=pl.ANY),
            *[
                pl.BlockSpec(one.shape, lambda i: (0, 0), pipeline_mode=pl.Buffered(1))
                for one in earlier
            ],
        ],
        out_specs=pl.BlockSpec((rows, wide), lambda i: (0, 0)),
        scratch_shapes=[
            pltpu.VMEM((heads, *w_uv.shape[1:]), jnp.bfloat16),
            pltpu.VMEM((KEY + P_SIZE, length), jnp.bfloat16),
            pltpu.VMEM((heads, rows, R), jnp.bfloat16),
            pltpu.VMEM((R // LANES, heads // SPLIT * tall, LANES), jnp.float32),
            pltpu.VMEM((tall, LANES), jnp.float32),
            pltpu.VMEM((rows, LANES), jnp.float32),
            pltpu.SemaphoreType.DMA((SPLIT,)),
        ],
        compiler_params=pltpu.CompilerParams(vmem_limit_bytes=56 << 20),
        cost_estimate=pl.CostEstimate(
            flops=2 * rows * heads * length * (KEY + R) + 2 * rows * heads * R * V,
            bytes_accessed=2 * (received.size + own.size + caches.size + heads * R * V + rows * wide),
            transcendentals=rows * heads * length,
        ),
        name="prefix",
    )(received, own, caches, w_uv, *earlier)


def merge_kernel(target_ref, answer_ref, value_ref, mass_ref, out_ref):
    forks, heads = mass_ref.shape
    group_heads = heads // SPLIT
    at = lax.broadcasted_iota(jnp.int32, (forks, answer_ref.shape[0]), 1)
    picking = (at == target_ref[...]).astype(jnp.bfloat16)

    def pick(start, size):
        return jnp.dot(
            picking, answer_ref[:, start : start + size], preferred_element_type=jnp.float32
        )

    begin = 0

    for lead, count in PARTS:
        run = 2 * count
        come = pick(begin + run * SPLIT * V, 2 * LANES)
        mass = come[:, :LANES] + come[:, LANES:]
        for n in range(SPLIT):
            first = n * group_heads + 2 * lead
            mass_prefix = mass[:, n * run : (n + 1) * run]
            mass_suffix = mass_ref[:, first : first + run]
            top = jnp.maximum(mass_prefix, mass_suffix)
            share_prefix = jnp.exp(mass_prefix - top)
            share_suffix = jnp.exp(mass_suffix - top)
            both = share_prefix + share_suffix
            part_prefix = share_prefix / both
            part_suffix = share_suffix / both
            value = pick(begin + n * run * V, run * V)
            for h in range(run):
                cut = slice((first + h) * V, (first + h + 1) * V)
                out_ref[:, cut] = (
                    part_prefix[:, h : h + 1] * value[:, h * V : (h + 1) * V]
                    + part_suffix[:, h : h + 1] * value_ref[:, cut].astype(jnp.float32)
                ).astype(out_ref.dtype)
        begin += run * SPLIT * V + 2 * LANES


def merge(target, answer, value_suffix, mass_suffix):
    forks = value_suffix.shape[0]
    return pl.pallas_call(
        merge_kernel,
        out_shape=jax.ShapeDtypeStruct((forks, value_suffix.shape[1]), jnp.bfloat16),
        compiler_params=pltpu.CompilerParams(vmem_limit_bytes=24 << 20),
        name="merge",
    )(target, answer, value_suffix, mass_suffix)


def suffix(queries, suffix_cache, suffix_len, w_uv):
    forks = queries.shape[0]
    heads = w_uv.shape[0]
    query_heads = queries.reshape(forks, heads, KEY)
    scores = (
        jnp.einsum("fhe,fes->fhs", query_heads, suffix_cache, preferred_element_type=jnp.float32)
        * SCALE
    )
    positions = jnp.arange(suffix_cache.shape[2], dtype=jnp.int32)
    live = (positions[None, :] < suffix_len[:, None])[:, None, :]
    scores = jnp.where(live, scores, -jnp.inf)
    peak = jnp.max(scores, axis=2, keepdims=True)
    weights = jnp.where(live, jnp.exp(scores - peak), 0.0)
    total = jnp.sum(weights, axis=2)
    summed = jnp.einsum(
        "fhs,frs->fhr",
        weights.astype(jnp.bfloat16),
        suffix_cache[:, :R, :],
        preferred_element_type=jnp.float32,
    )
    latent = (summed / total[..., None]).astype(jnp.bfloat16)
    value = jnp.einsum("nhr,hrv->nhv", latent, w_uv, preferred_element_type=jnp.float32)
    return value.astype(jnp.bfloat16).reshape(forks, heads * V), peak[..., 0] + jnp.log(total)


def shards(queries, prefix_cache, suffix_cache, w_uv, fork_prompt, prompt_slot, suffix_len):
    near = ("zl", "xc")
    group = lax.axis_size("zl") * lax.axis_size("xc")
    held = COPIES * MOST
    back = (lax.axis_index("zh") - prompt_slot // group) % COPIES
    base = ((prompt_slot % group) * held + back * MOST)[None, :].astype(jnp.int32)

    def from_behind(steps):
        return lax.ppermute(
            prefix_cache, "zh", [(n, (n + steps) % COPIES) for n in range(COPIES)]
        )

    def exchange(value):
        return lax.all_to_all(
            value.reshape(group, -1, value.shape[1]), near, split_axis=0, concat_axis=0, tiled=True
        )

    own = lax.all_gather(prefix_cache, "tp", axis=0, tiled=True)
    moved = [from_behind(n) for n in range(1, COPIES)]
    outbound, targets = zip(*[place(fork_prompt, base, queries, group, part) for part in PARTS])
    outbound = list(outbound)
    outbound[0], own, *moved = lax.optimization_barrier((outbound[0], own, *moved))
    caches = lax.all_gather(jnp.stack(moved, axis=1), "tp", axis=0, tiled=True)
    value_suffix, mass_suffix = suffix(queries, suffix_cache, suffix_len, w_uv)
    received = [exchange(outbound[0])]
    outbound[1], value_suffix, mass_suffix = lax.optimization_barrier(
        (outbound[1], value_suffix, mass_suffix)
    )
    received.append(exchange(outbound[1]))
    result = prefix(received[0], own, caches, w_uv, PARTS[0])
    result = prefix(received[1], own, caches, w_uv, PARTS[1], result)
    answer = exchange(result).reshape(result.shape)
    return merge(targets[0], answer, value_suffix, mass_suffix)


def solution(mesh):
    owners = mesh.shape["dp"]
    tp = mesh.shape["tp"]
    group = owners // COPIES
    devices = mesh.devices.reshape(COPIES, 2, group // 2, tp)
    split = Mesh(devices, ("zh", "zl", "xc", "tp"))
    dp = ("zh", "zl", "xc")
    placed = (
        P(dp, "tp"),
        P(dp, None, "tp"),
        P(dp, None, None),
        P("tp", None, None),
        P(dp, None),
        P(),
        P(dp),
    )
    return jax.shard_map(
        shards, mesh=split, in_specs=placed, out_specs=P(dp, "tp"), check_vma=False
    )
```

```python
import functools

import jax
import jax.numpy as jnp
from jax import lax
from jax.experimental import pallas as pl
from jax.experimental.pallas import tpu as pltpu
from jax.sharding import Mesh
from jax.sharding import PartitionSpec as P

R = 512
P_SIZE = 64
V = 128
KEY = R + P_SIZE
MOST = 2
COPIES = 4
SPLIT = 4
PARTS = ((0, 2), (2, 2))
CHUNKS = 2
LANES = 128
SCALE = 192.0 ** (-0.5)
LOG2E = 1.4426950408889634


def row_targets(prompt_col, base_row):
    forks = prompt_col.shape[0]
    prompts = base_row.shape[1]
    ids = lax.broadcasted_iota(jnp.int32, (forks, prompts), 1)
    base = jnp.sum(jnp.where(prompt_col == ids, base_row, 0), axis=1, keepdims=True)
    down = lax.broadcasted_iota(jnp.int32, (forks, forks), 0)
    along = lax.broadcasted_iota(jnp.int32, (forks, forks), 1)

    def turned(column):
        return jnp.sum(jnp.where(down == along, column, 0), axis=0, keepdims=True)

    before = (base == turned(base)) & (along < down)
    target = base + jnp.sum(before.astype(jnp.int32), axis=1, keepdims=True)
    return turned(target), target


def place_kernel(prompt_ref, base_ref, *refs):
    parts = refs[:SPLIT]
    out_ref, target_ref, placing_ref = refs[SPLIT:]
    forks = parts[0].shape[0]

    @pl.when(pl.program_id(0) == 0)
    def _():
        target_row, target_ref[...] = row_targets(prompt_ref[...], base_ref[...])
        at = lax.broadcasted_iota(jnp.int32, (out_ref.shape[0], forks), 0)
        for n in range(SPLIT):
            placing_ref[:, n * forks : (n + 1) * forks] = (at == target_row * SPLIT + n).astype(
                jnp.bfloat16
            )

    def paired(part):
        odd = part[:, KEY:]
        return jnp.concatenate([part[:, :R], odd[:, :R], part[:, R:KEY], odd[:, R:]], axis=1)

    stacked = jnp.concatenate([paired(part[...]) for part in parts], axis=0)
    out_ref[...] = jnp.dot(
        placing_ref[...], stacked, preferred_element_type=jnp.float32
    ).astype(jnp.bfloat16)


def place(prompt, base, queries, group, part):
    forks, width = queries.shape
    rows = group * COPIES * MOST * SPLIT
    tile = 2 * KEY
    steps = width // SPLIT // tile
    first, mine = part

    def part_spec(n):
        return pl.BlockSpec((forks, tile), lambda i: (0, n * steps + first + i))

    return pl.pallas_call(
        place_kernel,
        out_shape=(
            jax.ShapeDtypeStruct((rows, mine * tile), jnp.bfloat16),
            jax.ShapeDtypeStruct((forks, 1), jnp.int32),
        ),
        grid=(mine,),
        in_specs=[
            pl.BlockSpec(prompt.shape, lambda i: (0, 0)),
            pl.BlockSpec(base.shape, lambda i: (0, 0)),
            *[part_spec(n) for n in range(SPLIT)],
        ],
        out_specs=(
            pl.BlockSpec((rows, tile), lambda i: (0, i)),
            pl.BlockSpec((forks, 1), lambda i: (0, 0)),
        ),
        scratch_shapes=[pltpu.VMEM((rows, SPLIT * forks), jnp.bfloat16)],
        name="place",
    )(prompt, base, *[queries] * SPLIT)


def prefix_kernel(part, q_ref, kv_ref, w_hbm, *refs):
    *earlier, out_ref, w_ref, key_ref, lat_ref, part_ref, cell_ref, mass_ref, sem = refs
    ahead_of_it = earlier[0].shape[1] if earlier else 0
    step = pl.program_id(0)
    last = pl.num_programs(0) - 1
    heads = w_ref.shape[0]
    group = q_ref.shape[0]
    held = COPIES * MOST
    quarter = kv_ref.shape[2]
    run = heads // SPLIT
    group_heads = w_hbm.shape[0] // SPLIT
    fetches = [
        pltpu.make_async_copy(
            w_hbm.at[pl.ds(n * group_heads + 2 * part[0], run)],
            w_ref.at[pl.ds(n * run, run)],
            sem.at[n],
        )
        for n in range(SPLIT)
    ]

    @pl.when(step == 0)
    def _():
        for fetch in fetches:
            fetch.start()
        if earlier:
            out_ref[:, :ahead_of_it] = earlier[0][...]

    for n in range(kv_ref.shape[0]):
        cut = slice(n * quarter, (n + 1) * quarter)
        key_ref[0:KEY, cut] = kv_ref[n]
        key_ref[KEY : KEY + P_SIZE, cut] = kv_ref[n, R:KEY, :]

    tall = group * MOST * SPLIT
    span = group * MOST
    pairs = heads // SPLIT // 2
    lane = lax.broadcasted_iota(jnp.int32, (tall, LANES), 1)
    cells = jnp.zeros((tall, LANES), jnp.float32)
    rows = pl.ds(pl.multiple_of(step * span, span), span)

    def piece(start, size):
        return q_ref[:, :, start : start + size].reshape(tall, size)

    def query(pair, odd):
        start = pair * 2 * KEY
        ropes = piece(start + 2 * R, LANES)
        mine = (lane >= P_SIZE) if odd else (lane < P_SIZE)
        return jnp.concatenate(
            [piece(start + odd * R, R), jnp.where(mine, ropes, jnp.zeros_like(ropes))], axis=1
        )

    order = [(pair, odd) for odd in range(2) for pair in range(pairs)]
    chunks = CHUNKS if len(order) > CHUNKS else 1
    per = len(order) // chunks

    def score(chunk):
        return jnp.dot(
            jnp.concatenate([query(*one) for one in order[chunk * per : (chunk + 1) * per]], axis=0),
            key_ref[...],
            preferred_element_type=jnp.float32,
        )

    ahead = [score(chunk) for chunk in range(1)]
    for chunk in range(chunks):
        scores = ahead.pop(0)
        if chunk + 1 < chunks:
            ahead.append(score(chunk + 1))
        peak = jnp.max(scores, axis=1, keepdims=True)
        weights = jnp.exp2((scores - peak) * (SCALE * LOG2E))
        total = jnp.sum(weights, axis=1, keepdims=True)
        summed = lax.dot_general(
            weights.astype(jnp.bfloat16),
            key_ref[0:R, :],
            (((1,), (1,)), ((), ())),
            preferred_element_type=jnp.float32,
        )
        latent = summed * (1.0 / total)
        for b in range(R // LANES):
            part_ref[b, chunk * per * tall : (chunk + 1) * per * tall, :] = latent[:, b * LANES : (b + 1) * LANES]
        mass = peak * SCALE + jnp.log(total)
        for at, (pair, odd) in enumerate(order[chunk * per : (chunk + 1) * per]):
            cells = jnp.where(lane == 2 * pair + odd, mass[at * tall : (at + 1) * tall], cells)
    for at, (pair, odd) in enumerate(order):
        for n in range(SPLIT):
            head = n * 2 * pairs + 2 * pair + odd
            for b in range(R // LANES):
                lat_ref[head, rows, b * LANES : (b + 1) * LANES] = part_ref[
                    b, pl.ds(at * tall + n, span, stride=SPLIT), :
                ].astype(jnp.bfloat16)
    cell_ref[...] = cells
    masses = jnp.zeros((span, LANES), jnp.float32)
    for n in range(SPLIT):
        block = cell_ref[pl.ds(n, span, stride=SPLIT), :]
        masses = masses + (pltpu.roll(block, n * 2 * pairs, 1) if n else block)
    mass_ref[rows, :] = masses

    @pl.when(step == last)
    def _():
        for fetch in fetches:
            fetch.wait()
        count = mass_ref.shape[0]
        to = lax.broadcasted_iota(jnp.int32, (count, count), 0)
        come = lax.broadcasted_iota(jnp.int32, (count, count), 1)
        source, slot = to // held, to % held
        turn = (come == (slot // MOST) * span + source * MOST + slot % MOST).astype(jnp.bfloat16)

        def put(at, block):
            begin = ahead_of_it + at
            out_ref[:, begin : begin + block.shape[1]] = jnp.dot(
                turn, block, preferred_element_type=jnp.float32
            ).astype(jnp.bfloat16)

        for head in range(0, heads, 2):
            both = [
                jnp.dot(lat_ref[h], w_ref[h], preferred_element_type=jnp.float32)
                for h in (head, head + 1)
            ]
            put(head * V, jnp.concatenate(both, axis=1).astype(jnp.bfloat16))
        high = mass_ref[...].astype(jnp.bfloat16)
        low = (mass_ref[...] - high.astype(jnp.float32)).astype(jnp.bfloat16)
        put(heads * V, jnp.concatenate([high, low], axis=1))


def prefix(received, caches, w_uv, part, *earlier):
    group, _, width = received.shape
    heads = 2 * part[1] * SPLIT
    rows = group * COPIES * MOST
    tall = group * MOST * SPLIT
    parts = caches.shape[0]
    length = parts * caches.shape[3]
    wide = heads * V + 2 * LANES + sum(one.shape[1] for one in earlier)
    return pl.pallas_call(
        functools.partial(prefix_kernel, part),
        out_shape=jax.ShapeDtypeStruct((rows, wide), jnp.bfloat16),
        grid=(COPIES,),
        in_specs=[
            pl.BlockSpec((group, MOST * SPLIT, width), lambda i: (0, i, 0)),
            pl.BlockSpec((parts, None, *caches.shape[2:]), lambda i: (0, i, 0, 0)),
            pl.BlockSpec(memory_space=pl.ANY),
            *[
                pl.BlockSpec(one.shape, lambda i: (0, 0), pipeline_mode=pl.Buffered(1))
                for one in earlier
            ],
        ],
        out_specs=pl.BlockSpec((rows, wide), lambda i: (0, 0)),
        scratch_shapes=[
            pltpu.VMEM((heads, *w_uv.shape[1:]), jnp.bfloat16),
            pltpu.VMEM((KEY + P_SIZE, length), jnp.bfloat16),
            pltpu.VMEM((heads, rows, R), jnp.bfloat16),
            pltpu.VMEM((R // LANES, heads // SPLIT * tall, LANES), jnp.float32),
            pltpu.VMEM((tall, LANES), jnp.float32),
            pltpu.VMEM((rows, LANES), jnp.float32),
            pltpu.SemaphoreType.DMA((SPLIT,)),
        ],
        compiler_params=pltpu.CompilerParams(vmem_limit_bytes=56 << 20),
        cost_estimate=pl.CostEstimate(
            flops=2 * rows * heads * length * (KEY + R) + 2 * rows * heads * R * V,
            bytes_accessed=2 * (received.size + caches.size + heads * R * V + rows * wide),
            transcendentals=rows * heads * length,
        ),
        name="prefix",
    )(received, caches, w_uv, *earlier)


def merge_kernel(target_ref, answer_ref, value_ref, mass_ref, out_ref):
    forks, heads = mass_ref.shape
    group_heads = heads // SPLIT
    at = lax.broadcasted_iota(jnp.int32, (forks, answer_ref.shape[0]), 1)
    picking = (at == target_ref[...]).astype(jnp.bfloat16)

    def pick(start, size):
        return jnp.dot(
            picking, answer_ref[:, start : start + size], preferred_element_type=jnp.float32
        )

    begin = 0

    for lead, count in PARTS:
        run = 2 * count
        come = pick(begin + run * SPLIT * V, 2 * LANES)
        mass = come[:, :LANES] + come[:, LANES:]
        for n in range(SPLIT):
            first = n * group_heads + 2 * lead
            mass_prefix = mass[:, n * run : (n + 1) * run]
            mass_suffix = mass_ref[:, first : first + run]
            top = jnp.maximum(mass_prefix, mass_suffix)
            share_prefix = jnp.exp(mass_prefix - top)
            share_suffix = jnp.exp(mass_suffix - top)
            both = share_prefix + share_suffix
            part_prefix = share_prefix / both
            part_suffix = share_suffix / both
            value = pick(begin + n * run * V, run * V)
            for h in range(run):
                cut = slice((first + h) * V, (first + h + 1) * V)
                out_ref[:, cut] = (
                    part_prefix[:, h : h + 1] * value[:, h * V : (h + 1) * V]
                    + part_suffix[:, h : h + 1] * value_ref[:, cut].astype(jnp.float32)
                ).astype(out_ref.dtype)
        begin += run * SPLIT * V + 2 * LANES


def merge(target, answer, value_suffix, mass_suffix):
    forks = value_suffix.shape[0]
    return pl.pallas_call(
        merge_kernel,
        out_shape=jax.ShapeDtypeStruct((forks, value_suffix.shape[1]), jnp.bfloat16),
        compiler_params=pltpu.CompilerParams(vmem_limit_bytes=24 << 20),
        name="merge",
    )(target, answer, value_suffix, mass_suffix)


def suffix(queries, suffix_cache, suffix_len, w_uv):
    forks = queries.shape[0]
    heads = w_uv.shape[0]
    query_heads = queries.reshape(forks, heads, KEY)
    scores = (
        jnp.einsum("fhe,fes->fhs", query_heads, suffix_cache, preferred_element_type=jnp.float32)
        * SCALE
    )
    positions = jnp.arange(suffix_cache.shape[2], dtype=jnp.int32)
    live = (positions[None, :] < suffix_len[:, None])[:, None, :]
    scores = jnp.where(live, scores, -jnp.inf)
    peak = jnp.max(scores, axis=2, keepdims=True)
    weights = jnp.where(live, jnp.exp(scores - peak), 0.0)
    total = jnp.sum(weights, axis=2)
    summed = jnp.einsum(
        "fhs,frs->fhr",
        weights.astype(jnp.bfloat16),
        suffix_cache[:, :R, :],
        preferred_element_type=jnp.float32,
    )
    latent = (summed / total[..., None]).astype(jnp.bfloat16)
    value = jnp.einsum("nhr,hrv->nhv", latent, w_uv, preferred_element_type=jnp.float32)
    return value.astype(jnp.bfloat16).reshape(forks, heads * V), peak[..., 0] + jnp.log(total)


def shards(queries, prefix_cache, suffix_cache, w_uv, fork_prompt, prompt_slot, suffix_len):
    near = ("zl", "xc")
    group = lax.axis_size("zl") * lax.axis_size("xc")
    held = COPIES * MOST
    back = (lax.axis_index("zh") - prompt_slot // group) % COPIES
    base = ((prompt_slot % group) * held + back * MOST)[None, :].astype(jnp.int32)

    def along(value, steps):
        return lax.ppermute(value, "zh", [(n, (n + steps) % COPIES) for n in range(COPIES)])

    def exchange(value):
        return lax.all_to_all(
            value.reshape(group, -1, value.shape[1]), near, split_axis=0, concat_axis=0, tiled=True
        )

    middle = prefix_cache.shape[1] // 2
    behind, before = along(prefix_cache, 1), along(prefix_cache, COPIES - 1)
    across = [along(behind[:, :middle], 1), along(before[:, middle:], COPIES - 1)]
    outbound, targets = zip(*[place(fork_prompt, base, queries, group, part) for part in PARTS])
    outbound = list(outbound)
    outbound[0], behind, before, *across = lax.optimization_barrier(
        (outbound[0], behind, before, *across)
    )
    held_here = [prefix_cache, behind, jnp.concatenate(across, axis=1), before]
    caches = lax.all_gather(jnp.stack(held_here, axis=1), "tp", axis=0, tiled=True)
    value_suffix, mass_suffix = suffix(queries, suffix_cache, suffix_len, w_uv)
    received = [exchange(outbound[0])]
    outbound[1], value_suffix, mass_suffix = lax.optimization_barrier(
        (outbound[1], value_suffix, mass_suffix)
    )
    received.append(exchange(outbound[1]))
    result = prefix(received[0], caches, w_uv, PARTS[0])
    result = prefix(received[1], caches, w_uv, PARTS[1], result)
    answer = exchange(result).reshape(result.shape)
    return merge(targets[0], answer, value_suffix, mass_suffix)


def solution(mesh):
    owners = mesh.shape["dp"]
    tp = mesh.shape["tp"]
    group = owners // COPIES
    devices = mesh.devices.reshape(COPIES, 2, group // 2, tp)
    split = Mesh(devices, ("zh", "zl", "xc", "tp"))
    dp = ("zh", "zl", "xc")
    placed = (
        P(dp, "tp"),
        P(dp, None, "tp"),
        P(dp, None, None),
        P("tp", None, None),
        P(dp, None),
        P(),
        P(dp),
    )
    return jax.shard_map(
        shards, mesh=split, in_specs=placed, out_specs=P(dp, "tp"), check_vma=False
    )
```

```python
import functools

import jax
import jax.numpy as jnp
from jax import lax
from jax.experimental import pallas as pl
from jax.experimental.pallas import tpu as pltpu
from jax.sharding import Mesh
from jax.sharding import PartitionSpec as P

R = 512
P_SIZE = 64
V = 128
KEY = R + P_SIZE
MOST = 2
COPIES = 4
SPLIT = 4
PARTS = ((0, 2), (2, 2))
CHUNKS = 2
LANES = 128
SCALE = 192.0 ** (-0.5)
LOG2E = 1.4426950408889634


def row_targets(prompt_col, base_row):
    forks = prompt_col.shape[0]
    prompts = base_row.shape[1]
    ids = lax.broadcasted_iota(jnp.int32, (forks, prompts), 1)
    base = jnp.sum(jnp.where(prompt_col == ids, base_row, 0), axis=1, keepdims=True)
    down = lax.broadcasted_iota(jnp.int32, (forks, forks), 0)
    along = lax.broadcasted_iota(jnp.int32, (forks, forks), 1)

    def turned(column):
        return jnp.sum(jnp.where(down == along, column, 0), axis=0, keepdims=True)

    before = (base == turned(base)) & (along < down)
    target = base + jnp.sum(before.astype(jnp.int32), axis=1, keepdims=True)
    return turned(target), target


def place_kernel(prompt_ref, base_ref, *refs):
    parts = refs[:SPLIT]
    out_ref, target_ref, placing_ref = refs[SPLIT:]
    forks = parts[0].shape[0]

    @pl.when(pl.program_id(0) == 0)
    def _():
        target_row, target_ref[...] = row_targets(prompt_ref[...], base_ref[...])
        at = lax.broadcasted_iota(jnp.int32, (out_ref.shape[0], forks), 0)
        for n in range(SPLIT):
            placing_ref[:, n * forks : (n + 1) * forks] = (at == target_row * SPLIT + n).astype(
                jnp.bfloat16
            )

    def paired(part):
        odd = part[:, KEY:]
        return jnp.concatenate([part[:, :R], odd[:, :R], part[:, R:KEY], odd[:, R:]], axis=1)

    stacked = jnp.concatenate([paired(part[...]) for part in parts], axis=0)
    out_ref[...] = jnp.dot(
        placing_ref[...], stacked, preferred_element_type=jnp.float32
    ).astype(jnp.bfloat16)


def place(prompt, base, queries, group, part):
    forks, width = queries.shape
    rows = group * COPIES * MOST * SPLIT
    tile = 2 * KEY
    steps = width // SPLIT // tile
    first, mine = part

    def part_spec(n):
        return pl.BlockSpec((forks, tile), lambda i: (0, n * steps + first + i))

    return pl.pallas_call(
        place_kernel,
        out_shape=(
            jax.ShapeDtypeStruct((rows, mine * tile), jnp.bfloat16),
            jax.ShapeDtypeStruct((forks, 1), jnp.int32),
        ),
        grid=(mine,),
        in_specs=[
            pl.BlockSpec(prompt.shape, lambda i: (0, 0)),
            pl.BlockSpec(base.shape, lambda i: (0, 0)),
            *[part_spec(n) for n in range(SPLIT)],
        ],
        out_specs=(
            pl.BlockSpec((rows, tile), lambda i: (0, i)),
            pl.BlockSpec((forks, 1), lambda i: (0, 0)),
        ),
        scratch_shapes=[pltpu.VMEM((rows, SPLIT * forks), jnp.bfloat16)],
        name="place",
    )(prompt, base, *[queries] * SPLIT)


def prefix_kernel(part, q_ref, kv_ref, w_hbm, out_ref, *scratch):
    w_ref, key_ref, lat_ref, part_ref, cell_ref, mass_ref, sem = scratch
    step = pl.program_id(0)
    last = pl.num_programs(0) - 1
    heads = w_ref.shape[0]
    group = q_ref.shape[0]
    held = COPIES * MOST
    quarter = kv_ref.shape[2]
    run = heads // SPLIT
    group_heads = w_hbm.shape[0] // SPLIT
    fetches = [
        pltpu.make_async_copy(
            w_hbm.at[pl.ds(n * group_heads + 2 * part[0], run)],
            w_ref.at[pl.ds(n * run, run)],
            sem.at[n],
        )
        for n in range(SPLIT)
    ]

    @pl.when(step == 0)
    def _():
        for fetch in fetches:
            fetch.start()

    for n in range(kv_ref.shape[0]):
        cut = slice(n * quarter, (n + 1) * quarter)
        key_ref[0:KEY, cut] = kv_ref[n]
        key_ref[KEY : KEY + P_SIZE, cut] = kv_ref[n, R:KEY, :]

    tall = group * MOST * SPLIT
    span = group * MOST
    pairs = heads // SPLIT // 2
    lane = lax.broadcasted_iota(jnp.int32, (tall, LANES), 1)
    cells = jnp.zeros((tall, LANES), jnp.float32)
    rows = pl.ds(pl.multiple_of(step * span, span), span)

    def piece(start, size):
        return q_ref[:, :, start : start + size].reshape(tall, size)

    def query(pair, odd):
        start = pair * 2 * KEY
        ropes = piece(start + 2 * R, LANES)
        mine = (lane >= P_SIZE) if odd else (lane < P_SIZE)
        return jnp.concatenate(
            [piece(start + odd * R, R), jnp.where(mine, ropes, jnp.zeros_like(ropes))], axis=1
        )

    order = [(pair, odd) for odd in range(2) for pair in range(pairs)]
    chunks = CHUNKS if len(order) > CHUNKS else 1
    per = len(order) // chunks

    def score(chunk):
        return jnp.dot(
            jnp.concatenate([query(*one) for one in order[chunk * per : (chunk + 1) * per]], axis=0),
            key_ref[...],
            preferred_element_type=jnp.float32,
        )

    ahead = [score(chunk) for chunk in range(1)]
    for chunk in range(chunks):
        scores = ahead.pop(0)
        if chunk + 1 < chunks:
            ahead.append(score(chunk + 1))
        peak = jnp.max(scores, axis=1, keepdims=True)
        weights = jnp.exp2((scores - peak) * (SCALE * LOG2E))
        total = jnp.sum(weights, axis=1, keepdims=True)
        summed = lax.dot_general(
            weights.astype(jnp.bfloat16),
            key_ref[0:R, :],
            (((1,), (1,)), ((), ())),
            preferred_element_type=jnp.float32,
        )
        latent = summed * (1.0 / total)
        for b in range(R // LANES):
            part_ref[b, chunk * per * tall : (chunk + 1) * per * tall, :] = latent[:, b * LANES : (b + 1) * LANES]
        mass = peak * SCALE + jnp.log(total)
        for at, (pair, odd) in enumerate(order[chunk * per : (chunk + 1) * per]):
            cells = jnp.where(lane == 2 * pair + odd, mass[at * tall : (at + 1) * tall], cells)
    for at, (pair, odd) in enumerate(order):
        for n in range(SPLIT):
            head = n * 2 * pairs + 2 * pair + odd
            for b in range(R // LANES):
                lat_ref[head, rows, b * LANES : (b + 1) * LANES] = part_ref[
                    b, pl.ds(at * tall + n, span, stride=SPLIT), :
                ].astype(jnp.bfloat16)
    cell_ref[...] = cells
    masses = jnp.zeros((span, LANES), jnp.float32)
    for n in range(SPLIT):
        block = cell_ref[pl.ds(n, span, stride=SPLIT), :]
        masses = masses + (pltpu.roll(block, n * 2 * pairs, 1) if n else block)
    mass_ref[rows, :] = masses

    @pl.when(step == last)
    def _():
        for fetch in fetches:
            fetch.wait()
        count = mass_ref.shape[0]
        to = lax.broadcasted_iota(jnp.int32, (count, count), 0)
        come = lax.broadcasted_iota(jnp.int32, (count, count), 1)
        source, slot = to // held, to % held
        turn = (come == (slot // MOST) * span + source * MOST + slot % MOST).astype(jnp.bfloat16)

        def put(at, block):
            out_ref[:, at : at + block.shape[1]] = jnp.dot(
                turn, block, preferred_element_type=jnp.float32
            ).astype(jnp.bfloat16)

        for head in range(0, heads, 2):
            both = [
                jnp.dot(lat_ref[h], w_ref[h], preferred_element_type=jnp.float32)
                for h in (head, head + 1)
            ]
            put(head * V, jnp.concatenate(both, axis=1).astype(jnp.bfloat16))
        high = mass_ref[...].astype(jnp.bfloat16)
        low = (mass_ref[...] - high.astype(jnp.float32)).astype(jnp.bfloat16)
        put(heads * V, jnp.concatenate([high, low], axis=1))


def prefix(received, caches, w_uv, part):
    group, _, width = received.shape
    heads = 2 * part[1] * SPLIT
    rows = group * COPIES * MOST
    tall = group * MOST * SPLIT
    parts = caches.shape[0]
    length = parts * caches.shape[3]
    wide = heads * V + 2 * LANES
    return pl.pallas_call(
        functools.partial(prefix_kernel, part),
        out_shape=jax.ShapeDtypeStruct((rows, wide), jnp.bfloat16),
        grid=(COPIES,),
        in_specs=[
            pl.BlockSpec((group, MOST * SPLIT, width), lambda i: (0, i, 0)),
            pl.BlockSpec((parts, None, *caches.shape[2:]), lambda i: (0, i, 0, 0)),
            pl.BlockSpec(memory_space=pl.ANY),
        ],
        out_specs=pl.BlockSpec((rows, wide), lambda i: (0, 0)),
        scratch_shapes=[
            pltpu.VMEM((heads, *w_uv.shape[1:]), jnp.bfloat16),
            pltpu.VMEM((KEY + P_SIZE, length), jnp.bfloat16),
            pltpu.VMEM((heads, rows, R), jnp.bfloat16),
            pltpu.VMEM((R // LANES, heads // SPLIT * tall, LANES), jnp.float32),
            pltpu.VMEM((tall, LANES), jnp.float32),
            pltpu.VMEM((rows, LANES), jnp.float32),
            pltpu.SemaphoreType.DMA((SPLIT,)),
        ],
        compiler_params=pltpu.CompilerParams(vmem_limit_bytes=62 << 20),
        cost_estimate=pl.CostEstimate(
            flops=2 * rows * heads * length * (KEY + R) + 2 * rows * heads * R * V,
            bytes_accessed=2 * (received.size + caches.size + heads * R * V + rows * wide),
            transcendentals=rows * heads * length,
        ),
        name="prefix",
    )(received, caches, w_uv)


def merge_kernel(target_ref, *refs):
    answers = refs[: len(PARTS)]
    value_ref, mass_ref, out_ref = refs[len(PARTS) :]
    forks, heads = mass_ref.shape
    group_heads = heads // SPLIT
    at = lax.broadcasted_iota(jnp.int32, (forks, answers[0].shape[0]), 1)
    picking = (at == target_ref[...]).astype(jnp.bfloat16)
    for (lead, count), answer in zip(PARTS, answers, strict=True):
        run = 2 * count
        come = jnp.dot(picking, answer[...], preferred_element_type=jnp.float32)
        masses = come[:, run * SPLIT * V :]
        mass = masses[:, :LANES] + masses[:, LANES:]
        for n in range(SPLIT):
            first = n * group_heads + 2 * lead
            mass_prefix = mass[:, n * run : (n + 1) * run]
            mass_suffix = mass_ref[:, first : first + run]
            top = jnp.maximum(mass_prefix, mass_suffix)
            share_prefix = jnp.exp(mass_prefix - top)
            share_suffix = jnp.exp(mass_suffix - top)
            both = share_prefix + share_suffix
            part_prefix = share_prefix / both
            part_suffix = share_suffix / both
            for h in range(run):
                cut = slice((first + h) * V, (first + h + 1) * V)
                come_at = (n * run + h) * V
                out_ref[:, cut] = (
                    part_prefix[:, h : h + 1] * come[:, come_at : come_at + V]
                    + part_suffix[:, h : h + 1] * value_ref[:, cut].astype(jnp.float32)
                ).astype(out_ref.dtype)


def merge(target, answers, value_suffix, mass_suffix):
    return pl.pallas_call(
        merge_kernel,
        out_shape=jax.ShapeDtypeStruct(value_suffix.shape, jnp.bfloat16),
        compiler_params=pltpu.CompilerParams(vmem_limit_bytes=24 << 20),
        name="merge",
    )(target, *answers, value_suffix, mass_suffix)


def suffix(queries, suffix_cache, suffix_len, w_uv):
    forks = queries.shape[0]
    heads = w_uv.shape[0]
    query_heads = queries.reshape(forks, heads, KEY)
    scores = (
        jnp.einsum("fhe,fes->fhs", query_heads, suffix_cache, preferred_element_type=jnp.float32)
        * SCALE
    )
    positions = jnp.arange(suffix_cache.shape[2], dtype=jnp.int32)
    live = (positions[None, :] < suffix_len[:, None])[:, None, :]
    scores = jnp.where(live, scores, -jnp.inf)
    peak = jnp.max(scores, axis=2, keepdims=True)
    weights = jnp.where(live, jnp.exp(scores - peak), 0.0)
    total = jnp.sum(weights, axis=2)
    summed = jnp.einsum(
        "fhs,frs->fhr",
        weights.astype(jnp.bfloat16),
        suffix_cache[:, :R, :],
        preferred_element_type=jnp.float32,
    )
    latent = (summed / total[..., None]).astype(jnp.bfloat16)
    value = jnp.einsum("nhr,hrv->nhv", latent, w_uv, preferred_element_type=jnp.float32)
    return value.astype(jnp.bfloat16).reshape(forks, heads * V), peak[..., 0] + jnp.log(total)


def shards(queries, prefix_cache, suffix_cache, w_uv, fork_prompt, prompt_slot, suffix_len):
    near = ("zl", "xc")
    group = lax.axis_size("zl") * lax.axis_size("xc")
    held = COPIES * MOST
    back = (lax.axis_index("zh") - prompt_slot // group) % COPIES
    base = ((prompt_slot % group) * held + back * MOST)[None, :].astype(jnp.int32)

    def along(value, steps):
        return lax.ppermute(value, "zh", [(n, (n + steps) % COPIES) for n in range(COPIES)])

    def exchange(value):
        return lax.all_to_all(
            value.reshape(group, -1, value.shape[1]), near, split_axis=0, concat_axis=0, tiled=True
        )

    middle = prefix_cache.shape[1] // 2
    behind, before = along(prefix_cache, 1), along(prefix_cache, COPIES - 1)
    across = [along(behind[:, :middle], 1), along(before[:, middle:], COPIES - 1)]
    outbound, targets = zip(*[place(fork_prompt, base, queries, group, part) for part in PARTS])
    outbound = list(outbound)
    outbound[0], behind, before, *across = lax.optimization_barrier(
        (outbound[0], behind, before, *across)
    )
    held_here = [prefix_cache, behind, jnp.concatenate(across, axis=1), before]
    caches = lax.all_gather(jnp.stack(held_here, axis=1), "tp", axis=0, tiled=True)
    value_suffix, mass_suffix = suffix(queries, suffix_cache, suffix_len, w_uv)
    received = [exchange(outbound[0])]
    outbound[1], value_suffix, mass_suffix = lax.optimization_barrier(
        (outbound[1], value_suffix, mass_suffix)
    )
    received.append(exchange(outbound[1]))
    results = [prefix(received[0], caches, w_uv, PARTS[0])]
    received[1], results[0] = lax.optimization_barrier((received[1], results[0]))
    answers = [exchange(results[0]).reshape(results[0].shape)]
    results.append(prefix(received[1], caches, w_uv, PARTS[1]))
    results[1], answers[0] = lax.optimization_barrier((results[1], answers[0]))
    answers.append(exchange(results[1]).reshape(results[1].shape))
    return merge(targets[0], answers, value_suffix, mass_suffix)


def solution(mesh):
    owners = mesh.shape["dp"]
    tp = mesh.shape["tp"]
    group = owners // COPIES
    devices = mesh.devices.reshape(COPIES, 2, group // 2, tp)
    split = Mesh(devices, ("zh", "zl", "xc", "tp"))
    dp = ("zh", "zl", "xc")
    placed = (
        P(dp, "tp"),
        P(dp, None, "tp"),
        P(dp, None, None),
        P("tp", None, None),
        P(dp, None),
        P(),
        P(dp),
    )
    return jax.shard_map(
        shards, mesh=split, in_specs=placed, out_specs=P(dp, "tp"), check_vma=False
    )
```

```python
import functools

import jax
import jax.numpy as jnp
from jax import lax
from jax.experimental import pallas as pl
from jax.experimental.pallas import tpu as pltpu
from jax.sharding import Mesh
from jax.sharding import PartitionSpec as P

R = 512
P_SIZE = 64
V = 128
KEY = R + P_SIZE
MOST = 2
COPIES = 4
SPLIT = 4
PARTS = ((0, 2), (2, 2))
CHUNKS = 2
LANES = 128
SCALE = 192.0 ** (-0.5)
LOG2E = 1.4426950408889634


def row_targets(prompt_col, base_row):
    forks = prompt_col.shape[0]
    prompts = base_row.shape[1]
    ids = lax.broadcasted_iota(jnp.int32, (forks, prompts), 1)
    base = jnp.sum(jnp.where(prompt_col == ids, base_row, 0), axis=1, keepdims=True)
    down = lax.broadcasted_iota(jnp.int32, (forks, forks), 0)
    along = lax.broadcasted_iota(jnp.int32, (forks, forks), 1)

    def turned(column):
        return jnp.sum(jnp.where(down == along, column, 0), axis=0, keepdims=True)

    before = (base == turned(base)) & (along < down)
    target = base + jnp.sum(before.astype(jnp.int32), axis=1, keepdims=True)
    return turned(target), target


def place_kernel(prompt_ref, base_ref, *refs):
    parts = refs[:SPLIT]
    out_ref, target_ref, placing_ref = refs[SPLIT:]
    forks = parts[0].shape[0]

    @pl.when(pl.program_id(0) == 0)
    def _():
        target_row, target_ref[...] = row_targets(prompt_ref[...], base_ref[...])
        at = lax.broadcasted_iota(jnp.int32, (out_ref.shape[0], forks), 0)
        for n in range(SPLIT):
            placing_ref[:, n * forks : (n + 1) * forks] = (at == target_row * SPLIT + n).astype(
                jnp.bfloat16
            )

    def paired(part):
        odd = part[:, KEY:]
        return jnp.concatenate([part[:, :R], odd[:, :R], part[:, R:KEY], odd[:, R:]], axis=1)

    stacked = jnp.concatenate([paired(part[...]) for part in parts], axis=0)
    out_ref[...] = jnp.dot(
        placing_ref[...], stacked, preferred_element_type=jnp.float32
    ).astype(jnp.bfloat16)


def place(prompt, base, queries, group, part):
    forks, width = queries.shape
    rows = group * COPIES * MOST * SPLIT
    tile = 2 * KEY
    steps = width // SPLIT // tile
    first, mine = part

    def part_spec(n):
        return pl.BlockSpec((forks, tile), lambda i: (0, n * steps + first + i))

    return pl.pallas_call(
        place_kernel,
        out_shape=(
            jax.ShapeDtypeStruct((rows, mine * tile), jnp.bfloat16),
            jax.ShapeDtypeStruct((forks, 1), jnp.int32),
        ),
        grid=(mine,),
        in_specs=[
            pl.BlockSpec(prompt.shape, lambda i: (0, 0)),
            pl.BlockSpec(base.shape, lambda i: (0, 0)),
            *[part_spec(n) for n in range(SPLIT)],
        ],
        out_specs=(
            pl.BlockSpec((rows, tile), lambda i: (0, i)),
            pl.BlockSpec((forks, 1), lambda i: (0, 0)),
        ),
        scratch_shapes=[pltpu.VMEM((rows, SPLIT * forks), jnp.bfloat16)],
        name="place",
    )(prompt, base, *[queries] * SPLIT)


def prefix_kernel(part, q_ref, kv_ref, w_hbm, out_ref, *scratch):
    w_ref, key_ref, lat_ref, part_ref, cell_ref, mass_ref, sem = scratch
    step = pl.program_id(0)
    last = pl.num_programs(0) - 1
    heads = w_ref.shape[0]
    group = q_ref.shape[0]
    held = COPIES * MOST
    quarter = kv_ref.shape[2]
    run = heads // SPLIT
    group_heads = w_hbm.shape[0] // SPLIT
    fetches = [
        pltpu.make_async_copy(
            w_hbm.at[pl.ds(n * group_heads + 2 * part[0], run)],
            w_ref.at[pl.ds(n * run, run)],
            sem.at[n],
        )
        for n in range(SPLIT)
    ]

    @pl.when(step == 0)
    def _():
        for fetch in fetches:
            fetch.start()

    for n in range(kv_ref.shape[0]):
        cut = slice(n * quarter, (n + 1) * quarter)
        key_ref[0:KEY, cut] = kv_ref[n]
        key_ref[KEY : KEY + P_SIZE, cut] = kv_ref[n, R:KEY, :]

    tall = group * MOST * SPLIT
    span = group * MOST
    pairs = heads // SPLIT // 2
    lane = lax.broadcasted_iota(jnp.int32, (tall, LANES), 1)
    cells = jnp.zeros((tall, LANES), jnp.float32)
    rows = pl.ds(pl.multiple_of(step * span, span), span)

    def piece(start, size):
        return q_ref[:, :, start : start + size].reshape(tall, size)

    def query(pair, odd):
        start = pair * 2 * KEY
        ropes = piece(start + 2 * R, LANES)
        mine = (lane >= P_SIZE) if odd else (lane < P_SIZE)
        return jnp.concatenate(
            [piece(start + odd * R, R), jnp.where(mine, ropes, jnp.zeros_like(ropes))], axis=1
        )

    order = [(pair, odd) for odd in range(2) for pair in range(pairs)]
    chunks = CHUNKS if len(order) > CHUNKS else 1
    per = len(order) // chunks

    def score(chunk):
        return jnp.dot(
            jnp.concatenate([query(*one) for one in order[chunk * per : (chunk + 1) * per]], axis=0),
            key_ref[...],
            preferred_element_type=jnp.float32,
        )

    ahead = [score(chunk) for chunk in range(1)]
    for chunk in range(chunks):
        scores = ahead.pop(0)
        if chunk + 1 < chunks:
            ahead.append(score(chunk + 1))
        peak = jnp.max(scores, axis=1, keepdims=True)
        weights = jnp.exp2((scores - peak) * (SCALE * LOG2E))
        total = jnp.sum(weights, axis=1, keepdims=True)
        summed = lax.dot_general(
            weights.astype(jnp.bfloat16),
            key_ref[0:R, :],
            (((1,), (1,)), ((), ())),
            preferred_element_type=jnp.float32,
        )
        latent = summed * (1.0 / total)
        for b in range(R // LANES):
            part_ref[b, chunk * per * tall : (chunk + 1) * per * tall, :] = latent[:, b * LANES : (b + 1) * LANES]
        mass = peak * SCALE + jnp.log(total)
        for at, (pair, odd) in enumerate(order[chunk * per : (chunk + 1) * per]):
            cells = jnp.where(lane == 2 * pair + odd, mass[at * tall : (at + 1) * tall], cells)
    for at, (pair, odd) in enumerate(order):
        for n in range(SPLIT):
            head = n * 2 * pairs + 2 * pair + odd
            for b in range(R // LANES):
                lat_ref[head, rows, b * LANES : (b + 1) * LANES] = part_ref[
                    b, pl.ds(at * tall + n, span, stride=SPLIT), :
                ].astype(jnp.bfloat16)
    cell_ref[...] = cells
    masses = jnp.zeros((span, LANES), jnp.float32)
    for n in range(SPLIT):
        block = cell_ref[pl.ds(n, span, stride=SPLIT), :]
        masses = masses + (pltpu.roll(block, n * 2 * pairs, 1) if n else block)
    mass_ref[rows, :] = masses

    @pl.when(step == last)
    def _():
        for fetch in fetches:
            fetch.wait()
        count = mass_ref.shape[0]
        to = lax.broadcasted_iota(jnp.int32, (count, count), 0)
        come = lax.broadcasted_iota(jnp.int32, (count, count), 1)
        source, slot = to // held, to % held
        turn = (come == (slot // MOST) * span + source * MOST + slot % MOST).astype(jnp.bfloat16)

        def put(at, block):
            out_ref[:, at : at + block.shape[1]] = jnp.dot(
                turn, block, preferred_element_type=jnp.float32
            ).astype(jnp.bfloat16)

        for head in range(0, heads, 2):
            both = [
                jnp.dot(lat_ref[h], w_ref[h], preferred_element_type=jnp.float32)
                for h in (head, head + 1)
            ]
            put(head * V, jnp.concatenate(both, axis=1).astype(jnp.bfloat16))
        high = mass_ref[...].astype(jnp.bfloat16)
        low = (mass_ref[...] - high.astype(jnp.float32)).astype(jnp.bfloat16)
        spot = lax.broadcasted_iota(jnp.int32, mass_ref.shape, 1)
        moved = pltpu.roll(low.astype(jnp.float32), LANES // 2, 1)
        put(heads * V, jnp.where(spot < LANES // 2, high.astype(jnp.float32), moved).astype(jnp.bfloat16))


def prefix(received, caches, w_uv, part):
    group, _, width = received.shape
    heads = 2 * part[1] * SPLIT
    rows = group * COPIES * MOST
    tall = group * MOST * SPLIT
    parts = caches.shape[0]
    length = parts * caches.shape[3]
    wide = heads * V + LANES
    return pl.pallas_call(
        functools.partial(prefix_kernel, part),
        out_shape=jax.ShapeDtypeStruct((rows, wide), jnp.bfloat16),
        grid=(COPIES,),
        in_specs=[
            pl.BlockSpec((group, MOST * SPLIT, width), lambda i: (0, i, 0)),
            pl.BlockSpec((parts, None, *caches.shape[2:]), lambda i: (0, i, 0, 0)),
            pl.BlockSpec(memory_space=pl.ANY),
        ],
        out_specs=pl.BlockSpec((rows, wide), lambda i: (0, 0)),
        scratch_shapes=[
            pltpu.VMEM((heads, *w_uv.shape[1:]), jnp.bfloat16),
            pltpu.VMEM((KEY + P_SIZE, length), jnp.bfloat16),
            pltpu.VMEM((heads, rows, R), jnp.bfloat16),
            pltpu.VMEM((R // LANES, heads // SPLIT * tall, LANES), jnp.float32),
            pltpu.VMEM((tall, LANES), jnp.float32),
            pltpu.VMEM((rows, LANES), jnp.float32),
            pltpu.SemaphoreType.DMA((SPLIT,)),
        ],
        compiler_params=pltpu.CompilerParams(vmem_limit_bytes=62 << 20),
        cost_estimate=pl.CostEstimate(
            flops=2 * rows * heads * length * (KEY + R) + 2 * rows * heads * R * V,
            bytes_accessed=2 * (received.size + caches.size + heads * R * V + rows * wide),
            transcendentals=rows * heads * length,
        ),
        name="prefix",
    )(received, caches, w_uv)


def merge_kernel(target_ref, *refs):
    answers = refs[: len(PARTS)]
    value_ref, mass_ref, out_ref = refs[len(PARTS) :]
    forks, heads = mass_ref.shape
    group_heads = heads // SPLIT
    at = lax.broadcasted_iota(jnp.int32, (forks, answers[0].shape[0]), 1)
    picking = (at == target_ref[...]).astype(jnp.bfloat16)
    done = 0
    for (lead, count), answer in zip(PARTS, answers, strict=True):
        run = 2 * count
        mine = run * SPLIT
        come = jnp.dot(picking, answer[...], preferred_element_type=jnp.float32)
        masses = come[:, mine * V :]
        mass_prefix = masses[:, :mine] + masses[:, LANES // 2 : LANES // 2 + mine]
        mass_suffix = mass_ref[:, done : done + mine]
        done += mine
        top = jnp.maximum(mass_prefix, mass_suffix)
        share_prefix = jnp.exp(mass_prefix - top)
        share_suffix = jnp.exp(mass_suffix - top)
        both = share_prefix + share_suffix
        part_prefix = share_prefix / both
        part_suffix = share_suffix / both
        for h in range(mine):
            head = h // run * group_heads + 2 * lead + h % run
            cut = slice(head * V, (head + 1) * V)
            out_ref[:, cut] = (
                part_prefix[:, h : h + 1] * come[:, h * V : (h + 1) * V]
                + part_suffix[:, h : h + 1] * value_ref[:, cut].astype(jnp.float32)
            ).astype(out_ref.dtype)


def merge(target, answers, value_suffix, mass_suffix):
    return pl.pallas_call(
        merge_kernel,
        out_shape=jax.ShapeDtypeStruct(value_suffix.shape, jnp.bfloat16),
        compiler_params=pltpu.CompilerParams(vmem_limit_bytes=24 << 20),
        name="merge",
    )(target, *answers, value_suffix, mass_suffix)


def suffix(queries, suffix_cache, suffix_len, w_uv):
    forks = queries.shape[0]
    heads = w_uv.shape[0]
    query_heads = queries.reshape(forks, heads, KEY)
    scores = (
        jnp.einsum("fhe,fes->fhs", query_heads, suffix_cache, preferred_element_type=jnp.float32)
        * SCALE
    )
    positions = jnp.arange(suffix_cache.shape[2], dtype=jnp.int32)
    live = (positions[None, :] < suffix_len[:, None])[:, None, :]
    scores = jnp.where(live, scores, -jnp.inf)
    peak = jnp.max(scores, axis=2, keepdims=True)
    weights = jnp.where(live, jnp.exp(scores - peak), 0.0)
    total = jnp.sum(weights, axis=2)
    summed = jnp.einsum(
        "fhs,frs->fhr",
        weights.astype(jnp.bfloat16),
        suffix_cache[:, :R, :],
        preferred_element_type=jnp.float32,
    )
    latent = (summed / total[..., None]).astype(jnp.bfloat16)
    value = jnp.einsum("nhr,hrv->nhv", latent, w_uv, preferred_element_type=jnp.float32)
    return value.astype(jnp.bfloat16).reshape(forks, heads * V), peak[..., 0] + jnp.log(total)


def shards(queries, prefix_cache, suffix_cache, w_uv, fork_prompt, prompt_slot, suffix_len):
    near = ("zl", "xc")
    group = lax.axis_size("zl") * lax.axis_size("xc")
    held = COPIES * MOST
    back = (lax.axis_index("zh") - prompt_slot // group) % COPIES
    base = ((prompt_slot % group) * held + back * MOST)[None, :].astype(jnp.int32)

    def along(value, steps):
        return lax.ppermute(value, "zh", [(n, (n + steps) % COPIES) for n in range(COPIES)])

    def exchange(value):
        return lax.all_to_all(
            value.reshape(group, -1, value.shape[1]), near, split_axis=0, concat_axis=0, tiled=True
        )

    middle = prefix_cache.shape[1] // 2
    behind, before = along(prefix_cache, 1), along(prefix_cache, COPIES - 1)
    across = [along(behind[:, :middle], 1), along(before[:, middle:], COPIES - 1)]
    outbound, targets = zip(*[place(fork_prompt, base, queries, group, part) for part in PARTS])
    outbound = list(outbound)
    outbound[0], behind, before, *across = lax.optimization_barrier(
        (outbound[0], behind, before, *across)
    )
    held_here = [prefix_cache, behind, jnp.concatenate(across, axis=1), before]
    caches = lax.all_gather(jnp.stack(held_here, axis=1), "tp", axis=0, tiled=True)
    value_suffix, mass_suffix = suffix(queries, suffix_cache, suffix_len, w_uv)
    grouped = mass_suffix.reshape(mass_suffix.shape[0], SPLIT, -1)
    mass_suffix = jnp.concatenate(
        [
            grouped[:, :, 2 * lead : 2 * (lead + count)].reshape(mass_suffix.shape[0], -1)
            for lead, count in PARTS
        ],
        axis=1,
    )
    received = [exchange(outbound[0])]
    outbound[1], value_suffix, mass_suffix = lax.optimization_barrier(
        (outbound[1], value_suffix, mass_suffix)
    )
    received.append(exchange(outbound[1]))
    results = [prefix(received[0], caches, w_uv, PARTS[0])]
    received[1], results[0] = lax.optimization_barrier((received[1], results[0]))
    answers = [exchange(results[0]).reshape(results[0].shape)]
    results.append(prefix(received[1], caches, w_uv, PARTS[1]))
    results[1], answers[0] = lax.optimization_barrier((results[1], answers[0]))
    answers.append(exchange(results[1]).reshape(results[1].shape))
    return merge(targets[0], answers, value_suffix, mass_suffix)


def solution(mesh):
    owners = mesh.shape["dp"]
    tp = mesh.shape["tp"]
    group = owners // COPIES
    devices = mesh.devices.reshape(COPIES, 2, group // 2, tp)
    split = Mesh(devices, ("zh", "zl", "xc", "tp"))
    dp = ("zh", "zl", "xc")
    placed = (
        P(dp, "tp"),
        P(dp, None, "tp"),
        P(dp, None, None),
        P("tp", None, None),
        P(dp, None),
        P(),
        P(dp),
    )
    return jax.shard_map(
        shards, mesh=split, in_specs=placed, out_specs=P(dp, "tp"), check_vma=False
    )
```

```python
import functools

import jax
import jax.numpy as jnp
from jax import lax
from jax.experimental import pallas as pl
from jax.experimental.pallas import tpu as pltpu
from jax.sharding import Mesh
from jax.sharding import PartitionSpec as P

R = 512
P_SIZE = 64
V = 128
KEY = R + P_SIZE
MOST = 2
COPIES = 4
SPLIT = 4
PARTS = ((0, 2), (2, 2))
CHUNKS = 2
LANES = 128
SCALE = 192.0 ** (-0.5)
LOG2E = 1.4426950408889634


def row_targets(prompt_col, base_row):
    forks = prompt_col.shape[0]
    prompts = base_row.shape[1]
    ids = lax.broadcasted_iota(jnp.int32, (forks, prompts), 1)
    base = jnp.sum(jnp.where(prompt_col == ids, base_row, 0), axis=1, keepdims=True)
    down = lax.broadcasted_iota(jnp.int32, (forks, forks), 0)
    along = lax.broadcasted_iota(jnp.int32, (forks, forks), 1)

    def turned(column):
        return jnp.sum(jnp.where(down == along, column, 0), axis=0, keepdims=True)

    before = (base == turned(base)) & (along < down)
    target = base + jnp.sum(before.astype(jnp.int32), axis=1, keepdims=True)
    return turned(target), target


def place_kernel(prompt_ref, base_ref, *refs):
    parts = refs[:SPLIT]
    out_ref, target_ref, placing_ref = refs[SPLIT:]
    forks = parts[0].shape[0]

    @pl.when(pl.program_id(0) == 0)
    def _():
        target_row, target_ref[...] = row_targets(prompt_ref[...], base_ref[...])
        at = lax.broadcasted_iota(jnp.int32, (out_ref.shape[0], forks), 0)
        for n in range(SPLIT):
            placing_ref[:, n * forks : (n + 1) * forks] = (at == target_row * SPLIT + n).astype(
                jnp.bfloat16
            )

    def paired(part):
        odd = part[:, KEY:]
        return jnp.concatenate([part[:, :R], odd[:, :R], part[:, R:KEY], odd[:, R:]], axis=1)

    stacked = jnp.concatenate([paired(part[...]) for part in parts], axis=0)
    out_ref[...] = jnp.dot(
        placing_ref[...], stacked, preferred_element_type=jnp.float32
    ).astype(jnp.bfloat16)


def place(prompt, base, queries, group, part):
    forks, width = queries.shape
    rows = group * COPIES * MOST * SPLIT
    tile = 2 * KEY
    steps = width // SPLIT // tile
    first, mine = part

    def part_spec(n):
        return pl.BlockSpec((forks, tile), lambda i: (0, n * steps + first + i))

    return pl.pallas_call(
        place_kernel,
        out_shape=(
            jax.ShapeDtypeStruct((rows, mine * tile), jnp.bfloat16),
            jax.ShapeDtypeStruct((forks, 1), jnp.int32),
        ),
        grid=(mine,),
        in_specs=[
            pl.BlockSpec(prompt.shape, lambda i: (0, 0)),
            pl.BlockSpec(base.shape, lambda i: (0, 0)),
            *[part_spec(n) for n in range(SPLIT)],
        ],
        out_specs=(
            pl.BlockSpec((rows, tile), lambda i: (0, i)),
            pl.BlockSpec((forks, 1), lambda i: (0, 0)),
        ),
        scratch_shapes=[pltpu.VMEM((rows, SPLIT * forks), jnp.bfloat16)],
        name="place",
    )(prompt, base, *[queries] * SPLIT)


def prefix_kernel(part, q_ref, kv_ref, w_hbm, out_ref, *scratch):
    w_ref, key_ref, lat_ref, part_ref, cell_ref, mass_ref, sem = scratch
    step = pl.program_id(0)
    last = pl.num_programs(0) - 1
    heads = w_ref.shape[0]
    group = q_ref.shape[0]
    held = COPIES * MOST
    quarter = kv_ref.shape[2]
    run = heads // SPLIT
    group_heads = w_hbm.shape[0] // SPLIT
    fetches = [
        pltpu.make_async_copy(
            w_hbm.at[pl.ds(n * group_heads + 2 * part[0], run)],
            w_ref.at[pl.ds(n * run, run)],
            sem.at[n],
        )
        for n in range(SPLIT)
    ]

    @pl.when(step == 0)
    def _():
        for fetch in fetches:
            fetch.start()

    for n in range(kv_ref.shape[0]):
        cut = slice(n * quarter, (n + 1) * quarter)
        key_ref[0:KEY, cut] = kv_ref[n]
        key_ref[KEY : KEY + P_SIZE, cut] = kv_ref[n, R:KEY, :]

    tall = group * MOST * SPLIT
    span = group * MOST
    pairs = heads // SPLIT // 2
    lane = lax.broadcasted_iota(jnp.int32, (tall, LANES), 1)
    cells = jnp.zeros((tall, LANES), jnp.float32)
    rows = pl.ds(pl.multiple_of(step * span, span), span)

    def piece(start, size):
        return q_ref[:, :, start : start + size].reshape(tall, size)

    def query(pair, odd):
        start = pair * 2 * KEY
        ropes = piece(start + 2 * R, LANES)
        mine = (lane >= P_SIZE) if odd else (lane < P_SIZE)
        return jnp.concatenate(
            [piece(start + odd * R, R), jnp.where(mine, ropes, jnp.zeros_like(ropes))], axis=1
        )

    order = [(pair, odd) for odd in range(2) for pair in range(pairs)]
    chunks = CHUNKS if len(order) > CHUNKS else 1
    per = len(order) // chunks

    def score(chunk):
        return jnp.dot(
            jnp.concatenate([query(*one) for one in order[chunk * per : (chunk + 1) * per]], axis=0),
            key_ref[...],
            preferred_element_type=jnp.float32,
        )

    ahead = [score(chunk) for chunk in range(1)]
    for chunk in range(chunks):
        scores = ahead.pop(0)
        if chunk + 1 < chunks:
            ahead.append(score(chunk + 1))
        peak = jnp.max(scores, axis=1, keepdims=True)
        weights = jnp.exp2((scores - peak) * (SCALE * LOG2E))
        total = jnp.sum(weights, axis=1, keepdims=True)
        summed = lax.dot_general(
            weights.astype(jnp.bfloat16),
            key_ref[0:R, :],
            (((1,), (1,)), ((), ())),
            preferred_element_type=jnp.float32,
        )
        latent = summed * (1.0 / total)
        for b in range(R // LANES):
            part_ref[b, chunk * per * tall : (chunk + 1) * per * tall, :] = latent[:, b * LANES : (b + 1) * LANES]
        mass = peak * SCALE + jnp.log(total)
        for at, (pair, odd) in enumerate(order[chunk * per : (chunk + 1) * per]):
            cells = jnp.where(lane == 2 * pair + odd, mass[at * tall : (at + 1) * tall], cells)
    for at, (pair, odd) in enumerate(order):
        for n in range(SPLIT):
            head = n * 2 * pairs + 2 * pair + odd
            for b in range(R // LANES):
                lat_ref[head, rows, b * LANES : (b + 1) * LANES] = part_ref[
                    b, pl.ds(at * tall + n, span, stride=SPLIT), :
                ].astype(jnp.bfloat16)
    cell_ref[...] = cells
    masses = jnp.zeros((span, LANES), jnp.float32)
    for n in range(SPLIT):
        block = cell_ref[pl.ds(n, span, stride=SPLIT), :]
        masses = masses + (pltpu.roll(block, n * 2 * pairs, 1) if n else block)
    mass_ref[rows, :] = masses

    @pl.when(step == last)
    def _():
        for fetch in fetches:
            fetch.wait()
        count = mass_ref.shape[0]
        to = lax.broadcasted_iota(jnp.int32, (count, count), 0)
        come = lax.broadcasted_iota(jnp.int32, (count, count), 1)
        source, slot = to // held, to % held
        turn = (come == (slot // MOST) * span + source * MOST + slot % MOST).astype(jnp.bfloat16)

        def put(at, block):
            out_ref[:, at : at + block.shape[1]] = jnp.dot(
                turn, block, preferred_element_type=jnp.float32
            ).astype(jnp.bfloat16)

        for head in range(0, heads, 4):
            several = [
                jnp.dot(lat_ref[h], w_ref[h], preferred_element_type=jnp.float32)
                for h in range(head, head + 4)
            ]
            put(head * V, jnp.concatenate(several, axis=1).astype(jnp.bfloat16))
        high = mass_ref[...].astype(jnp.bfloat16)
        low = (mass_ref[...] - high.astype(jnp.float32)).astype(jnp.bfloat16)
        spot = lax.broadcasted_iota(jnp.int32, mass_ref.shape, 1)
        moved = pltpu.roll(low.astype(jnp.float32), LANES // 2, 1)
        put(heads * V, jnp.where(spot < LANES // 2, high.astype(jnp.float32), moved).astype(jnp.bfloat16))


def prefix(received, caches, w_uv, part):
    group, _, width = received.shape
    heads = 2 * part[1] * SPLIT
    rows = group * COPIES * MOST
    tall = group * MOST * SPLIT
    parts = caches.shape[0]
    length = parts * caches.shape[3]
    wide = heads * V + LANES
    return pl.pallas_call(
        functools.partial(prefix_kernel, part),
        out_shape=jax.ShapeDtypeStruct((rows, wide), jnp.bfloat16),
        grid=(COPIES,),
        in_specs=[
            pl.BlockSpec((group, MOST * SPLIT, width), lambda i: (0, i, 0)),
            pl.BlockSpec((parts, None, *caches.shape[2:]), lambda i: (0, i, 0, 0)),
            pl.BlockSpec(memory_space=pl.ANY),
        ],
        out_specs=pl.BlockSpec((rows, wide), lambda i: (0, 0)),
        scratch_shapes=[
            pltpu.VMEM((heads, *w_uv.shape[1:]), jnp.bfloat16),
            pltpu.VMEM((KEY + P_SIZE, length), jnp.bfloat16),
            pltpu.VMEM((heads, rows, R), jnp.bfloat16),
            pltpu.VMEM((R // LANES, heads // SPLIT * tall, LANES), jnp.float32),
            pltpu.VMEM((tall, LANES), jnp.float32),
            pltpu.VMEM((rows, LANES), jnp.float32),
            pltpu.SemaphoreType.DMA((SPLIT,)),
        ],
        compiler_params=pltpu.CompilerParams(vmem_limit_bytes=62 << 20),
        cost_estimate=pl.CostEstimate(
            flops=2 * rows * heads * length * (KEY + R) + 2 * rows * heads * R * V,
            bytes_accessed=2 * (received.size + caches.size + heads * R * V + rows * wide),
            transcendentals=rows * heads * length,
        ),
        name="prefix",
    )(received, caches, w_uv)


def merge_kernel(target_ref, *refs):
    answers = refs[: len(PARTS)]
    value_ref, mass_ref, out_ref = refs[len(PARTS) :]
    forks, heads = mass_ref.shape
    group_heads = heads // SPLIT
    at = lax.broadcasted_iota(jnp.int32, (forks, answers[0].shape[0]), 1)
    picking = (at == target_ref[...]).astype(jnp.bfloat16)
    done = 0
    for (lead, count), answer in zip(PARTS, answers, strict=True):
        run = 2 * count
        mine = run * SPLIT
        come = jnp.dot(picking, answer[...], preferred_element_type=jnp.float32)
        masses = come[:, mine * V :]
        mass_prefix = masses[:, :mine] + masses[:, LANES // 2 : LANES // 2 + mine]
        mass_suffix = mass_ref[:, done : done + mine]
        done += mine
        top = jnp.maximum(mass_prefix, mass_suffix)
        share_prefix = jnp.exp(mass_prefix - top)
        share_suffix = jnp.exp(mass_suffix - top)
        both = share_prefix + share_suffix
        part_prefix = share_prefix / both
        part_suffix = share_suffix / both
        for h in range(mine):
            head = h // run * group_heads + 2 * lead + h % run
            cut = slice(head * V, (head + 1) * V)
            out_ref[:, cut] = (
                part_prefix[:, h : h + 1] * come[:, h * V : (h + 1) * V]
                + part_suffix[:, h : h + 1] * value_ref[:, cut].astype(jnp.float32)
            ).astype(out_ref.dtype)


def merge(target, answers, value_suffix, mass_suffix):
    return pl.pallas_call(
        merge_kernel,
        out_shape=jax.ShapeDtypeStruct(value_suffix.shape, jnp.bfloat16),
        compiler_params=pltpu.CompilerParams(vmem_limit_bytes=24 << 20),
        name="merge",
    )(target, *answers, value_suffix, mass_suffix)


def suffix(queries, suffix_cache, suffix_len, w_uv):
    forks = queries.shape[0]
    heads = w_uv.shape[0]
    query_heads = queries.reshape(forks, heads, KEY)
    scores = (
        jnp.einsum("fhe,fes->fhs", query_heads, suffix_cache, preferred_element_type=jnp.float32)
        * SCALE
    )
    positions = jnp.arange(suffix_cache.shape[2], dtype=jnp.int32)
    live = (positions[None, :] < suffix_len[:, None])[:, None, :]
    scores = jnp.where(live, scores, -jnp.inf)
    peak = jnp.max(scores, axis=2, keepdims=True)
    weights = jnp.where(live, jnp.exp(scores - peak), 0.0)
    total = jnp.sum(weights, axis=2)
    summed = jnp.einsum(
        "fhs,frs->fhr",
        weights.astype(jnp.bfloat16),
        suffix_cache[:, :R, :],
        preferred_element_type=jnp.float32,
    )
    latent = (summed / total[..., None]).astype(jnp.bfloat16)
    value = jnp.einsum("nhr,hrv->nhv", latent, w_uv, preferred_element_type=jnp.float32)
    return value.astype(jnp.bfloat16).reshape(forks, heads * V), peak[..., 0] + jnp.log(total)


def shards(queries, prefix_cache, suffix_cache, w_uv, fork_prompt, prompt_slot, suffix_len):
    near = ("zl", "xc")
    group = lax.axis_size("zl") * lax.axis_size("xc")
    held = COPIES * MOST
    back = (lax.axis_index("zh") - prompt_slot // group) % COPIES
    base = ((prompt_slot % group) * held + back * MOST)[None, :].astype(jnp.int32)

    def along(value, steps):
        return lax.ppermute(value, "zh", [(n, (n + steps) % COPIES) for n in range(COPIES)])

    def exchange(value):
        return lax.all_to_all(
            value.reshape(group, -1, value.shape[1]), near, split_axis=0, concat_axis=0, tiled=True
        )

    middle = prefix_cache.shape[1] // 2
    behind, before = along(prefix_cache, 1), along(prefix_cache, COPIES - 1)
    across = [along(behind[:, :middle], 1), along(before[:, middle:], COPIES - 1)]
    outbound, targets = zip(*[place(fork_prompt, base, queries, group, part) for part in PARTS])
    outbound = list(outbound)
    outbound[0], behind, before, *across = lax.optimization_barrier(
        (outbound[0], behind, before, *across)
    )
    held_here = [prefix_cache, behind, jnp.concatenate(across, axis=1), before]
    caches = lax.all_gather(jnp.stack(held_here, axis=1), "tp", axis=0, tiled=True)
    value_suffix, mass_suffix = suffix(queries, suffix_cache, suffix_len, w_uv)
    grouped = mass_suffix.reshape(mass_suffix.shape[0], SPLIT, -1)
    mass_suffix = jnp.concatenate(
        [
            grouped[:, :, 2 * lead : 2 * (lead + count)].reshape(mass_suffix.shape[0], -1)
            for lead, count in PARTS
        ],
        axis=1,
    )
    received = [exchange(outbound[0])]
    outbound[1], value_suffix, mass_suffix = lax.optimization_barrier(
        (outbound[1], value_suffix, mass_suffix)
    )
    received.append(exchange(outbound[1]))
    results = [prefix(received[0], caches, w_uv, PARTS[0])]
    received[1], results[0] = lax.optimization_barrier((received[1], results[0]))
    answers = [exchange(results[0]).reshape(results[0].shape)]
    results.append(prefix(received[1], caches, w_uv, PARTS[1]))
    results[1], answers[0] = lax.optimization_barrier((results[1], answers[0]))
    answers.append(exchange(results[1]).reshape(results[1].shape))
    return merge(targets[0], answers, value_suffix, mass_suffix)


def solution(mesh):
    owners = mesh.shape["dp"]
    tp = mesh.shape["tp"]
    group = owners // COPIES
    devices = mesh.devices.reshape(COPIES, 2, group // 2, tp)
    split = Mesh(devices, ("zh", "zl", "xc", "tp"))
    dp = ("zh", "zl", "xc")
    placed = (
        P(dp, "tp"),
        P(dp, None, "tp"),
        P(dp, None, None),
        P("tp", None, None),
        P(dp, None),
        P(),
        P(dp),
    )
    return jax.shard_map(
        shards, mesh=split, in_specs=placed, out_specs=P(dp, "tp"), check_vma=False
    )
```
